768 devices in a mesh: ctx: 16 (over z_hi, x), fsdp: 48 (over z_lo, y, core).
Axes of the slice: x: 4, y: 8, z: 12 (z_hi: 4, z_lo: 3; z = z_hi * 3 + z_lo), core: 2. Of those that a mesh axis runs over, the one named last changes fastest.
Arguments:
- queries: bfloat16 [98304, 2048], P(('ctx', 'fsdp')), may hold values from -8 to 8
- keys: bfloat16 [98304, 1024], P(('ctx', 'fsdp')), may hold values from -8 to 8
- values: bfloat16 [98304, 1024], P(('ctx', 'fsdp')), may hold values from -6 to 6
- grad_out: bfloat16 [98304, 2048], P(('ctx', 'fsdp')), may hold values from -6 to 6
- segment: int32 [98304], P(('ctx', 'fsdp')), may hold values from 0 to 191, never falling along the last dimension, each value on 1 to 2048 neighbouring positions
Outputs:
- grad_queries: bfloat16 [98304, 2048], P(('ctx', 'fsdp'))
- grad_keys: bfloat16 [98304, 1024], P(('ctx', 'fsdp'))
- grad_values: bfloat16 [98304, 1024], P(('ctx', 'fsdp'))
The draws below stay inside these ranges and needn't reach their ends.
Inputs may be any that keep to these rules, and one draw needn't show every extreme that they name: `segment`: document ids never fall along the sequence; every document holds 1 to 2048 tokens and one holds exactly 2048.
All inputs are finite; a program needn't handle non-finite values.
Results may differ from the reference program's by a relative error of at most 0.0071.
Values may be sent and summed in bfloat16 or wider, within the bound.
A program may use at most 32 MiB of HBM per device.

```python
import math
import jax
import jax.numpy as jnp
import numpy as np
from jax import lax

HEADS = 16
KV_HEADS = 8
HEAD_DIM = 128
WINDOW = 512
TOK_DEV = 128
TOKENS = 98304
DOCS = 192
DOC_MOST = 2048


def block_scale(key, extent, pieces, low, top_value):
    def one(position, shards_of):
        draws = jax.random.uniform(jax.random.fold_in(jax.random.fold_in(key, 6), position), (shards_of,), jnp.float32, low / len(pieces), top_value / len(pieces))
        return jnp.repeat(jnp.exp(draws), extent[position] // shards_of).reshape((-1,) + (1,) * (len(extent) - position - 1))

    gain = one(*pieces[0])
    for cut in pieces[1:]:
        gain = gain * one(*cut)
    return gain


def split_up(amount, total, most, slope):
    portions = [(1 << 20) // math.isqrt(grade ** slope) + 1 for grade in range(2, amount + 1)]
    spare, counts = total - most - (amount - 1), [1] * (amount - 1)
    while spare > 0:
        candidates = [i for i in range(amount - 1) if counts[i] < most]
        whole, left = sum([portions[i] for i in candidates]), spare
        for i in candidates:
            addition = min(most - counts[i], max(1, left * portions[i] // whole), spare)
            counts[i] = counts[i] + addition
            spare = spare - addition
    return np.array([most] + counts)


def ragged_sizes(own_key, count, total, most, slope):
    if count == 2:
        one = jax.random.randint(own_key, (), max(1, total - most), min(most, total - 1) + 1)
        return jnp.stack([one, total - one])
    tallies = jnp.asarray(split_up(count, total, most, slope), jnp.int32)
    pairs = (count - 1) // 2
    donor, sink = tallies[1:1 + 2 * pairs:2], tallies[2:2 + 2 * pairs:2]
    slack = jnp.minimum(donor - 1, most - sink)
    shifted = jax.random.randint(jax.random.fold_in(own_key, 1), (pairs,), 0, 1 << 20) % (slack + 1)
    tallies = tallies.at[1:1 + 2 * pairs:2].set(donor - shifted).at[2:2 + 2 * pairs:2].set(sink + shifted)
    return tallies[jax.random.permutation(jax.random.fold_in(own_key, 2), count)]


def noise(stream_key, shape, scale, limit, shards=(), kind=jnp.bfloat16):
    values = scale * jax.random.normal(stream_key, shape, jnp.float32)
    if shards:
        values = values * block_scale(stream_key, shape, shards, -0.22, 0.18)
    return jnp.clip(values, -limit, limit).astype(kind)


def setup_inputs(seed: int = 0) -> dict:
    key_list = jax.random.split(jax.random.key(seed), 6)
    return {
        "queries": noise(key_list[0], (TOKENS, HEADS * HEAD_DIM), 2.0, 8.0, ((0, 768),)),
        "keys": noise(key_list[1], (TOKENS, KV_HEADS * HEAD_DIM), 2.0, 8.0, ((0, 768),)),
        "values": noise(key_list[2], (TOKENS, KV_HEADS * HEAD_DIM), 1.0, 6.0, ((0, 768),)),
        "grad_out": noise(key_list[3], (TOKENS, HEADS * HEAD_DIM), 1.0, 6.0, ((0, 768),)),
        "segment": jnp.searchsorted(jnp.cumsum(ragged_sizes(key_list[4], DOCS, TOKENS, DOC_MOST, 2)), jnp.arange(TOKENS), side="right").astype(jnp.int32),
    }


softcap = 50.0
inv_scale = 1.0 / 12.0


def tile_grads(query_rows, key_rows, value_rows, grad_rows, visible):
    raw_scores = jnp.einsum('ngrd,mgd->grnm', query_rows, key_rows)
    capped = softcap * jnp.tanh(raw_scores * inv_scale / softcap)
    weights = jnp.where(visible[None, None], jnp.exp(capped), jnp.float32(0.0))
    totals = jnp.sum(weights, axis=-1, keepdims=True)
    probs = weights / totals
    probs_low = lax.optimization_barrier(probs.astype(jnp.bfloat16)).astype(jnp.float32)
    attended = jnp.einsum('grnm,mgd->ngrd', probs_low, value_rows)
    row_terms = jnp.transpose(jnp.sum(grad_rows * attended, axis=-1), (1, 2, 0))[..., None]
    dprobs = jnp.einsum('ngrd,mgd->grnm', grad_rows, value_rows)
    dscore = probs * (dprobs - row_terms) * (1.0 - (capped / softcap) ** 2) * inv_scale
    dscore_low = lax.optimization_barrier(dscore.astype(jnp.bfloat16)).astype(jnp.float32)
    grad_q = jnp.einsum('grnm,mgd->ngrd', dscore_low, key_rows)
    grad_k = jnp.einsum('grnm,ngrd->mgd', dscore_low, query_rows)
    grad_v = jnp.einsum('grnm,ngrd->mgd', probs_low, grad_rows)
    return grad_q, grad_k, grad_v


def reference(queries, keys, values, grad_out, segment):
    reach = (WINDOW + TOK_DEV - 1) // TOK_DEV
    padding = reach * TOK_DEV
    group_size = HEADS // KV_HEADS
    kv_width = KV_HEADS * HEAD_DIM
    block_count = TOKENS // TOK_DEV
    keys_pad = jnp.concatenate([jnp.zeros((padding, kv_width), keys.dtype), keys], 0)
    values_pad = jnp.concatenate([jnp.zeros((padding, kv_width), values.dtype), values], 0)
    segment_pad = jnp.concatenate([-jnp.ones((padding,), jnp.int32), segment.astype(jnp.int32)], 0)
    row_index = jnp.arange(TOK_DEV, dtype=jnp.int32)
    col_index = jnp.arange(padding + TOK_DEV, dtype=jnp.int32)
    offsets = row_index[:, None] + padding - col_index[None, :]

    def advance(carry, block):
        grad_k_acc, grad_v_acc = carry
        start_row = (block * TOK_DEV).astype(jnp.int32)
        query_rows = lax.dynamic_slice_in_dim(queries, start_row, TOK_DEV, 0).astype(jnp.float32)
        query_rows = query_rows.reshape(TOK_DEV, KV_HEADS, group_size, HEAD_DIM)
        grad_rows = lax.dynamic_slice_in_dim(grad_out, start_row, TOK_DEV, 0).astype(jnp.float32)
        grad_rows = grad_rows.reshape(TOK_DEV, KV_HEADS, group_size, HEAD_DIM)
        key_rows = lax.dynamic_slice_in_dim(keys_pad, start_row, padding + TOK_DEV, 0).astype(jnp.float32)
        key_rows = key_rows.reshape(padding + TOK_DEV, KV_HEADS, HEAD_DIM)
        value_rows = lax.dynamic_slice_in_dim(values_pad, start_row, padding + TOK_DEV, 0).astype(jnp.float32)
        value_rows = value_rows.reshape(padding + TOK_DEV, KV_HEADS, HEAD_DIM)
        seg_query = lax.dynamic_slice_in_dim(segment, start_row, TOK_DEV, 0)
        seg_key = lax.dynamic_slice_in_dim(segment_pad, start_row, padding + TOK_DEV, 0)
        visible = (seg_query[:, None] == seg_key[None, :]) & (offsets >= 0) & (offsets < WINDOW)
        grad_q, grad_k, grad_v = tile_grads(query_rows, key_rows, value_rows, grad_rows, visible)
        old_k = lax.dynamic_slice_in_dim(grad_k_acc, start_row, padding + TOK_DEV, 0)
        old_v = lax.dynamic_slice_in_dim(grad_v_acc, start_row, padding + TOK_DEV, 0)
        grad_k_acc = lax.dynamic_update_slice_in_dim(grad_k_acc, old_k + grad_k.reshape(-1, kv_width), start_row, 0)
        grad_v_acc = lax.dynamic_update_slice_in_dim(grad_v_acc, old_v + grad_v.reshape(-1, kv_width), start_row, 0)
        return (grad_k_acc, grad_v_acc), grad_q.reshape(TOK_DEV, HEADS * HEAD_DIM).astype(jnp.bfloat16)

    zero_acc = jnp.zeros((TOKENS + padding, kv_width), jnp.float32)
    (grad_k_acc, grad_v_acc), grad_q_blocks = lax.scan(advance, (zero_acc, zero_acc), jnp.arange(block_count, dtype=jnp.int32))
    grad_queries = grad_q_blocks.reshape(TOKENS, HEADS * HEAD_DIM)
    return (grad_queries, grad_k_acc[padding:].astype(jnp.bfloat16), grad_v_acc[padding:].astype(jnp.bfloat16))
```

```python
import functools

import jax
import jax.numpy as jnp
from jax import lax
from jax.experimental import pallas as pl
from jax.experimental.pallas import tpu as pltpu
from jax.sharding import PartitionSpec as P

TOK = 128
DIM = 128
WINDOW = 512
KVH = 4
GROUP = 2
KVW = KVH * DIM
QW = KVW * GROUP
CHIP = 2 * TOK
REACH = WINDOW // TOK
ROWS = WINDOW + CHIP
SPAN = WINDOW + TOK
CAP = 50.0
SCALE = 1.0 / 12.0

NT = (((1,), (1,)), ((), ()))
NN = (((1,), (0,)), ((), ()))
TN = (((0,), (0,)), ((), ()))


def mm(lhs, rhs, dims):
    return lax.dot_general(lhs, rhs, dims, preferred_element_type=jnp.float32)


def kernel(
    chips,
    fsdp,
    q_hbm,
    k_hbm,
    v_hbm,
    do_hbm,
    seg_hbm,
    dq_hbm,
    dk_hbm,
    dv_hbm,
    kv,
    q,
    do,
    seg,
    mask,
    part,
    far_out,
    far_in,
    near_out,
    near_in,
    dq,
    dkv,
    own_send,
    own_recv,
    relay_send,
    relay_recv,
    swap_send,
    swap_recv,
    seg_send,
    seg_recv,
    seg_relay_send,
    seg_relay_recv,
    far_send,
    far_recv,
    near_send,
    near_recv,
    dq_send,
    dq_recv,
    dkv_send,
    dkv_recv,
):
    index = lax.axis_index("ctx") * fsdp + lax.axis_index("fsdp")
    chip = index // 2
    me = index % 2
    other = 1 - me

    def device(which_chip, core):
        at = which_chip * 2 + core
        return (at // fsdp, at % fsdp)

    ahead = (chip + 1) % chips
    behind = (chip + chips - 1) % chips
    partner = device(chip, other)

    def remote(src, dst, send, recv, to):
        return pltpu.make_async_remote_copy(
            src_ref=src,
            dst_ref=dst,
            send_sem=send,
            recv_sem=recv,
            device_id=to,
            device_id_type=pl.DeviceIdType.MESH,
        )

    def wait(ref, sem):
        pltpu.make_async_copy(ref, ref, sem).wait()

    def lanes(start, size):
        return pl.ds(pl.multiple_of(start, DIM), size)

    def rows(core, base=0):
        return pl.ds(pl.multiple_of(base + core * TOK, TOK), TOK)

    barrier = pltpu.get_barrier_semaphore()
    for to in (
        partner,
        device(ahead, 0),
        device(ahead, 1),
        device(behind, 0),
        device(behind, 1),
    ):
        pl.semaphore_signal(barrier, inc=1, device_id=to, device_id_type=pl.DeviceIdType.MESH)
    pl.semaphore_wait(barrier, 5)

    def send_own(j):
        for core in range(2):
            for which, src in ((0, k_hbm), (1, v_hbm)):
                remote(
                    src.at[:, lanes(core * KVW + j * DIM, DIM)],
                    kv.at[which, rows(me, CHIP), lanes(j * DIM, DIM)],
                    own_send.at[j],
                    own_recv.at[j],
                    device(ahead, core),
                ).start()

    def head_rows(start, j):
        return kv.at[:, start : start + CHIP, lanes(j * DIM, DIM)]

    def relay(j):
        wait(head_rows(CHIP, j), own_recv.at[j])
        remote(
            head_rows(CHIP, j),
            head_rows(0, j),
            relay_send.at[j],
            relay_recv.at[j],
            device(ahead, me),
        ).start()

    for core in range(2):
        remote(
            seg_hbm, seg.at[2 + me], seg_send, seg_recv, device(ahead, core)
        ).start()
    send_own(0)
    send_own(1)
    remote(seg_hbm, seg.at[REACH + me], seg_send, seg_recv, partner).start()
    pltpu.make_async_copy(seg_hbm, seg.at[REACH + me], seg_recv).start()
    swaps = (
        (k_hbm, kv.at[0, rows(me, WINDOW), :], KVW),
        (v_hbm, kv.at[1, rows(me, WINDOW), :], KVW),
        (q_hbm, q.at[rows(me), :], QW),
        (do_hbm, do.at[rows(me), :], QW),
    )
    for n, (src, dst, width) in enumerate(swaps):
        remote(
            src.at[:, lanes(other * width, width)],
            dst,
            swap_send.at[n],
            swap_recv.at[n],
            partner,
        ).start()
        pltpu.make_async_copy(
            src.at[:, lanes(me * width, width)], dst, swap_recv.at[n]
        ).start()

    wait(seg.at[2:6], seg_recv)
    remote(
        seg.at[2:4], seg.at[0:2], seg_relay_send, seg_relay_recv, device(ahead, me)
    ).start()
    for j in range(2):
        relay(j)
        send_own(j + 2)

    wait(seg.at[0:2], seg_relay_recv)
    key_at = lax.broadcasted_iota(jnp.int32, (TOK, TOK), 0)
    query_at = lax.broadcasted_iota(jnp.int32, (TOK, TOK), 1)
    for b in range(6):
        wide = jnp.broadcast_to(seg[b].astype(jnp.float32), (TOK, TOK))
        key_seg = wide.T
        real = jnp.where(2 * chip - REACH + b >= 0, 1.0, 0.0)
        for s in range(2):
            distance = REACH + s - b
            if distance < 0 or distance > REACH:
                continue
            query_seg = jnp.broadcast_to(seg[REACH + s].astype(jnp.float32), (TOK, TOK))
            seen = jnp.where(key_seg == query_seg, real, 0.0)
            if distance == 0:
                seen = jnp.where(query_at >= key_at, seen, 0.0)
            if distance == REACH:
                seen = jnp.where(query_at < key_at, seen, 0.0)
            at = (b - s) * TOK
            mask[s, at : at + TOK, :] = seen

    wait(kv.at[0, WINDOW:ROWS, :], swap_recv.at[0])
    wait(kv.at[1, WINDOW:ROWS, :], swap_recv.at[1])
    wait(q, swap_recv.at[2])
    wait(do, swap_recv.at[3])

    def unit(j, s):
        cols = lanes(j * DIM, DIM)
        keys = kv[0, s * TOK : s * TOK + SPAN, cols]
        vals = kv[1, s * TOK : s * TOK + SPAN, cols]

        def stacked(ref):
            return jnp.concatenate(
                [
                    ref[s * TOK : (s + 1) * TOK, lanes((j * GROUP + r) * DIM, DIM)]
                    for r in range(GROUP)
                ],
                axis=0,
            )

        queries = stacked(q)
        grads = stacked(do)
        seen = jnp.concatenate([mask[s]] * GROUP, axis=1)
        t = jnp.tanh(mm(keys, queries, NT) * (SCALE / CAP))
        weights = jnp.exp(CAP * t) * seen
        total = jnp.sum(weights, axis=0, keepdims=True)
        probs = weights * (1.0 / total)
        probs_low = probs.astype(jnp.bfloat16)
        dprobs = mm(vals, grads, NT)
        row_term = jnp.sum(probs_low.astype(jnp.float32) * dprobs, axis=0, keepdims=True)
        dscore = probs * (dprobs - row_term) * ((1.0 - t * t) * SCALE)
        dscore_low = dscore.astype(jnp.bfloat16)
        grad_k = mm(dscore_low, queries, NN)
        grad_v = mm(probs_low, grads, NN)
        grad_q = mm(keys, dscore_low, TN).T
        for r in range(GROUP):
            dq[s * TOK : (s + 1) * TOK, lanes((j * GROUP + r) * DIM, DIM)] = grad_q[
                r * TOK : (r + 1) * TOK
            ].astype(jnp.bfloat16)
        return grad_k, grad_v

    def far_copy(j):
        return remote(
            far_out.at[j], far_in.at[j], far_send.at[j], far_recv.at[j], device(behind, me)
        )

    def near_copy(j):
        return remote(
            near_out.at[j], near_in.at[j], near_send.at[j], near_recv.at[j], device(behind, me)
        )

    def pass_on(j):
        wait(far_in.at[j], far_recv.at[j])
        near_out[j] = (part[j, :, 0:CHIP, :] + far_in[j].astype(jnp.float32)).astype(jnp.bfloat16)
        near_copy(j).start()

    def swap_dq(j):
        width = GROUP * DIM
        into = lanes(me * QW + j * width, width)
        cols = lanes(j * width, width)
        remote(
            dq.at[rows(other), cols], dq_hbm.at[:, into], dq_send.at[j], dq_recv.at[j], partner
        ).start()
        pltpu.make_async_copy(dq.at[rows(me), cols], dq_hbm.at[:, into], dq_recv.at[j]).start()

    def finish(j):
        wait(near_in.at[j], near_recv.at[j])
        dkv[:, :, lanes(j * DIM, DIM)] = (
            part[j, :, CHIP:WINDOW, :] + near_in[j].astype(jnp.float32)
        ).astype(jnp.bfloat16)
        cols = lanes(j * DIM, DIM)
        into = lanes(me * KVW + j * DIM, DIM)
        for which, out in ((0, dk_hbm), (1, dv_hbm)):
            remote(
                dkv.at[which, rows(other), cols],
                out.at[:, into],
                dkv_send.at[which, j],
                dkv_recv.at[which, j],
                partner,
            ).start()
            pltpu.make_async_copy(
                dkv.at[which, rows(me), cols], out.at[:, into], dkv_recv.at[which, j]
            ).start()

    @pl.loop(0, KVH)
    def _(j):
        wait(head_rows(0, j), relay_recv.at[j])
        first = unit(j, 0)
        second = unit(j, 1)
        for which in range(2):
            low, high = first[which], second[which]
            far_out[j, which, 0:TOK, :] = low[0:TOK].astype(jnp.bfloat16)
            far_out[j, which, TOK:CHIP, :] = (low[TOK:CHIP] + high[0:TOK]).astype(jnp.bfloat16)
            part[j, which, 0 : WINDOW - TOK, :] = low[CHIP:SPAN] + high[TOK:WINDOW]
            part[j, which, WINDOW - TOK : WINDOW, :] = high[WINDOW:SPAN]
        far_copy(j).start()
        swap_dq(j)

        @pl.when(j < 2)
        def _():
            relay(j + 2)

        @pl.when(j >= 1)
        def _():
            pass_on(j - 1)

    pass_on(KVH - 1)

    @pl.loop(0, KVH)
    def _(j):
        finish(j)

    wait(seg.at[2:5], seg_send)
    wait(seg.at[2:4], seg_relay_send)
    for n, (_, dst, _) in enumerate(swaps):
        wait(dst, swap_send.at[n])

    @pl.loop(0, KVH)
    def _(j):
        width = GROUP * DIM
        wait(head_rows(CHIP, j), own_send.at[j])
        wait(head_rows(0, j), relay_send.at[j])
        wait(far_out.at[j], far_send.at[j])
        wait(near_out.at[j], near_send.at[j])
        wait(dq.at[0:TOK, lanes(j * width, width)], dq_send.at[j])
        wait(dq.at[:, lanes(j * width, width)], dq_recv.at[j])
        for which in range(2):
            wait(dkv.at[which, 0:TOK, lanes(j * DIM, DIM)], dkv_send.at[which, j])
            wait(dkv.at[which, :, lanes(j * DIM, DIM)], dkv_recv.at[which, j])


def local(chips, fsdp, queries, keys, values, grad_out, segment):
    low = jnp.bfloat16
    dma = pltpu.SemaphoreType.DMA
    anywhere = pl.BlockSpec(memory_space=pl.ANY)
    return pl.pallas_call(
        functools.partial(kernel, chips, fsdp),
        out_shape=(
            jax.ShapeDtypeStruct(queries.shape, low),
            jax.ShapeDtypeStruct(keys.shape, low),
            jax.ShapeDtypeStruct(values.shape, low),
        ),
        in_specs=[anywhere] * 5,
        out_specs=(anywhere,) * 3,
        scratch_shapes=[
            pltpu.VMEM((2, ROWS, KVW), low),
            pltpu.VMEM((CHIP, QW), low),
            pltpu.VMEM((CHIP, QW), low),
            pltpu.VMEM((6, 1, TOK), jnp.int32),
            pltpu.VMEM((2, SPAN, TOK), jnp.float32),
            pltpu.VMEM((KVH, 2, WINDOW, DIM), jnp.float32),
            pltpu.VMEM((KVH, 2, CHIP, DIM), low),
            pltpu.VMEM((KVH, 2, CHIP, DIM), low),
            pltpu.VMEM((KVH, 2, CHIP, DIM), low),
            pltpu.VMEM((KVH, 2, CHIP, DIM), low),
            pltpu.VMEM((CHIP, QW), low),
            pltpu.VMEM((2, CHIP, KVW), low),
            dma((KVH,)),
            dma((KVH,)),
            dma((KVH,)),
            dma((KVH,)),
            dma((4,)),
            dma((4,)),
            dma(()),
            dma(()),
            dma(()),
            dma(()),
            dma((KVH,)),
            dma((KVH,)),
            dma((KVH,)),
            dma((KVH,)),
            dma((KVH,)),
            dma((KVH,)),
            dma((2, KVH)),
            dma((2, KVH)),
        ],
        compiler_params=pltpu.CompilerParams(collective_id=0, has_side_effects=True),
        name="window_grads",
    )(queries, keys, values, grad_out, segment.reshape(1, TOK))


def solution(mesh):
    fsdp = mesh.shape["fsdp"]
    chips = mesh.shape["ctx"] * fsdp // 2
    split = P(("ctx", "fsdp"), None)
    return jax.shard_map(
        functools.partial(local, chips, fsdp),
        mesh=mesh,
        in_specs=(split, split, split, split, P(("ctx", "fsdp"))),
        out_specs=(split, split, split),
        check_vma=False,
    )
```

```python
import functools

import jax
import jax.numpy as jnp
from jax import lax
from jax.experimental import pallas as pl
from jax.experimental.pallas import tpu as pltpu
from jax.sharding import PartitionSpec as P

TOK = 128
DIM = 128
WINDOW = 512
KVH = 4
GROUP = 2
KVW = KVH * DIM
QW = KVW * GROUP
CHIP = 2 * TOK
REACH = WINDOW // TOK
ROWS = WINDOW + CHIP
SPAN = WINDOW + TOK
CAP = 50.0
SCALE = 1.0 / 12.0

NT = (((1,), (1,)), ((), ()))
NN = (((1,), (0,)), ((), ()))
TN = (((0,), (0,)), ((), ()))


def mm(lhs, rhs, dims):
    return lax.dot_general(lhs, rhs, dims, preferred_element_type=jnp.float32)


def kernel(
    chips,
    fsdp,
    q_hbm,
    k_hbm,
    v_hbm,
    do_hbm,
    seg_hbm,
    dq_out,
    near_in,
    own_in,
    kv,
    q,
    do,
    seg,
    mask,
    part,
    own_out,
    far_out,
    far_in,
    near_out,
    dq,
    own_send,
    own_recv,
    relay_send,
    relay_recv,
    swap_send,
    swap_recv,
    seg_send,
    seg_recv,
    seg_swap_send,
    seg_swap_recv,
    seg_relay_send,
    seg_relay_recv,
    far_send,
    far_recv,
    near_send,
    near_recv,
    dq_send,
    dq_recv,
    part_send,
    part_recv,
    ready,
):
    index = lax.axis_index("ctx") * fsdp + lax.axis_index("fsdp")
    chip = index // 2
    me = index % 2
    other = 1 - me

    def device(which_chip, core):
        at = which_chip * 2 + core
        return (at // fsdp, at % fsdp)

    ahead = (chip + 1) % chips
    behind = (chip + chips - 1) % chips
    partner = device(chip, other)

    def remote(src, dst, send, recv, to):
        return pltpu.make_async_remote_copy(
            src_ref=src,
            dst_ref=dst,
            send_sem=send,
            recv_sem=recv,
            device_id=to,
            device_id_type=pl.DeviceIdType.MESH,
        )

    def wait(ref, sem):
        pltpu.make_async_copy(ref, ref, sem).wait()

    def lanes(start, size):
        return pl.ds(pl.multiple_of(start, DIM), size)

    def rows(core, base=0):
        return pl.ds(pl.multiple_of(base + core * TOK, TOK), TOK)

    has_ahead = chip < chips - 1
    has_behind = chip > 0
    has_far = chip > 1

    def signal(sem, to):
        pl.semaphore_signal(sem, inc=1, device_id=to, device_id_type=pl.DeviceIdType.MESH)

    barrier = pltpu.get_barrier_semaphore()
    signal(barrier, partner)

    @pl.when(has_behind)
    def _():
        signal(barrier, device(behind, 0))
        signal(barrier, device(behind, 1))

    pl.semaphore_wait(barrier, 1 + 2 * jnp.where(has_ahead, 1, 0))

    @pl.when(has_ahead)
    def _():
        signal(ready, device(ahead, 0))
        signal(ready, device(ahead, 1))

    def send_own(j):
        for core in range(2):
            for which, src in ((0, k_hbm), (1, v_hbm)):
                remote(
                    src.at[:, lanes(core * KVW + j * DIM, DIM)],
                    kv.at[which, rows(me, CHIP), lanes(j * DIM, DIM)],
                    own_send.at[j],
                    own_recv.at[j],
                    device(ahead, core),
                ).start()

    def head_rows(start, j):
        return kv.at[:, start : start + CHIP, lanes(j * DIM, DIM)]

    def relay(j):
        @pl.when(has_behind)
        def _():
            wait(head_rows(CHIP, j), own_recv.at[j])

        @pl.when(has_behind & has_ahead)
        def _():
            remote(
                head_rows(CHIP, j),
                head_rows(0, j),
                relay_send.at[j],
                relay_recv.at[j],
                device(ahead, me),
            ).start()

    @pl.when(has_ahead)
    def _():
        for core in range(2):
            remote(seg_hbm, seg.at[2 + me], seg_send, seg_recv, device(ahead, core)).start()
        send_own(0)
        send_own(1)

    @pl.when(chip <= 1)
    def _():
        send_own(2)
        send_own(3)

    remote(seg_hbm, seg.at[REACH + me], seg_swap_send, seg_swap_recv, partner).start()
    pltpu.make_async_copy(seg_hbm, seg.at[REACH + me], seg_swap_recv).start()
    swaps = (
        (k_hbm, kv.at[0, rows(me, WINDOW), :], KVW),
        (v_hbm, kv.at[1, rows(me, WINDOW), :], KVW),
        (q_hbm, q.at[rows(me), :], QW),
        (do_hbm, do.at[rows(me), :], QW),
    )
    for n, (src, dst, width) in enumerate(swaps):
        remote(
            src.at[:, lanes(other * width, width)],
            dst,
            swap_send.at[n],
            swap_recv.at[n],
            partner,
        ).start()
        pltpu.make_async_copy(
            src.at[:, lanes(me * width, width)], dst, swap_recv.at[n]
        ).start()

    @pl.when(chip <= 1)
    def _():
        kv[:, 0:CHIP, :] = jnp.zeros((2, CHIP, KVW), kv.dtype)
        seg[0:2] = jnp.zeros((2, 1, TOK), seg.dtype)

    @pl.when(chip == 0)
    def _():
        kv[:, CHIP:WINDOW, :] = jnp.zeros((2, CHIP, KVW), kv.dtype)
        seg[2:4] = jnp.zeros((2, 1, TOK), seg.dtype)

    @pl.when(chip == chips - 1)
    def _():
        far_in[...] = jnp.zeros(far_in.shape, far_in.dtype)
        near_in[...] = jnp.zeros(near_in.shape, near_in.dtype)

    @pl.when(has_behind)
    def _():
        wait(seg.at[2:4], seg_recv)

    @pl.when(has_behind & has_ahead)
    def _():
        remote(
            seg.at[2:4], seg.at[0:2], seg_relay_send, seg_relay_recv, device(ahead, me)
        ).start()

    relay(0)
    relay(1)

    @pl.when(has_ahead & has_far)
    def _():
        send_own(2)
        send_own(3)

    wait(seg.at[4:6], seg_swap_recv)

    @pl.when(has_far)
    def _():
        wait(seg.at[0:2], seg_relay_recv)

    @pl.when(has_behind)
    def _():
        pl.semaphore_wait(ready, 2)

    key_at = lax.broadcasted_iota(jnp.int32, (TOK, TOK), 0)
    query_at = lax.broadcasted_iota(jnp.int32, (TOK, TOK), 1)
    for b in range(6):
        wide = jnp.broadcast_to(seg[b].astype(jnp.float32), (TOK, TOK))
        key_seg = wide.T
        real = jnp.where(2 * chip - REACH + b >= 0, 1.0, 0.0)
        for s in range(2):
            distance = REACH + s - b
            if distance < 0 or distance > REACH:
                continue
            query_seg = jnp.broadcast_to(seg[REACH + s].astype(jnp.float32), (TOK, TOK))
            seen = jnp.where(key_seg == query_seg, real, 0.0)
            if distance == 0:
                seen = jnp.where(query_at >= key_at, seen, 0.0)
            if distance == REACH:
                seen = jnp.where(query_at < key_at, seen, 0.0)
            at = (b - s) * TOK
            mask[s, at : at + TOK, :] = seen

    wait(kv.at[0, WINDOW:ROWS, :], swap_recv.at[0])
    wait(kv.at[1, WINDOW:ROWS, :], swap_recv.at[1])
    wait(q, swap_recv.at[2])
    wait(do, swap_recv.at[3])

    def unit(j, s):
        cols = lanes(j * DIM, DIM)
        keys = kv[0, s * TOK : s * TOK + SPAN, cols]
        vals = kv[1, s * TOK : s * TOK + SPAN, cols]

        def stacked(ref):
            return jnp.concatenate(
                [
                    ref[s * TOK : (s + 1) * TOK, lanes((j * GROUP + r) * DIM, DIM)]
                    for r in range(GROUP)
                ],
                axis=0,
            )

        queries = stacked(q)
        grads = stacked(do)
        seen = jnp.concatenate([mask[s]] * GROUP, axis=1)
        t = jnp.tanh(mm(keys, queries, NT) * (SCALE / CAP))
        weights = jnp.exp(CAP * t) * seen
        total = jnp.sum(weights, axis=0, keepdims=True)
        probs = weights * (1.0 / total)
        probs_low = probs.astype(jnp.bfloat16)
        dprobs = mm(vals, grads, NT)
        row_term = jnp.sum(probs_low.astype(jnp.float32) * dprobs, axis=0, keepdims=True)
        dscore = probs * (dprobs - row_term) * ((1.0 - t * t) * SCALE)
        dscore_low = dscore.astype(jnp.bfloat16)
        grad_k = mm(dscore_low, queries, NN)
        grad_v = mm(probs_low, grads, NN)
        grad_q = mm(keys, dscore_low, TN).T
        for r in range(GROUP):
            dq[s * TOK : (s + 1) * TOK, lanes((j * GROUP + r) * DIM, DIM)] = grad_q[
                r * TOK : (r + 1) * TOK
            ].astype(jnp.bfloat16)
        return grad_k, grad_v

    def far_copy(j):
        return remote(
            far_out.at[j], far_in.at[j], far_send.at[j], far_recv.at[j], device(behind, me)
        )

    def send_near(j):
        for core in range(2):
            remote(
                near_out.at[j, :, core * TOK : (core + 1) * TOK, :],
                near_in.at[:, :, lanes(me * KVW + j * DIM, DIM)],
                near_send.at[j],
                near_recv.at[me * KVH + j],
                device(behind, core),
            ).start()

    def pass_on(j):
        @pl.when(has_behind)
        def _():
            @pl.when(has_ahead)
            def _():
                wait(far_in.at[j], far_recv.at[j])

            near_out[j] = (part[j] + far_in[j].astype(jnp.float32)).astype(
                jnp.bfloat16
            )
            send_near(j)

    def swap(j):
        width = GROUP * DIM
        into = lanes(me * QW + j * width, width)
        cols = lanes(j * width, width)
        remote(
            dq.at[rows(other), cols], dq_out.at[:, into], dq_send.at[j], dq_recv.at[j], partner
        ).start()
        pltpu.make_async_copy(dq.at[rows(me), cols], dq_out.at[:, into], dq_recv.at[j]).start()
        into = lanes(me * KVW + j * DIM, DIM)
        remote(
            own_out.at[j, :, rows(other), :],
            own_in.at[:, :, into],
            part_send.at[j],
            part_recv.at[j],
            partner,
        ).start()
        pltpu.make_async_copy(
            own_out.at[j, :, rows(me), :], own_in.at[:, :, into], part_recv.at[j]
        ).start()

    @pl.loop(0, KVH)
    def _(j):
        @pl.when(has_far)
        def _():
            wait(head_rows(0, j), relay_recv.at[j])

        first = unit(j, 0)
        second = unit(j, 1)
        for which in range(2):
            low, high = first[which], second[which]
            far_out[j, which, 0:TOK, :] = low[0:TOK].astype(jnp.bfloat16)
            far_out[j, which, TOK:CHIP, :] = (low[TOK:CHIP] + high[0:TOK]).astype(jnp.bfloat16)
            part[j, which] = low[CHIP:WINDOW] + high[TOK : WINDOW - TOK]
            own_out[j, which, 0:TOK, :] = low[WINDOW:SPAN] + high[WINDOW - TOK : WINDOW]
            own_out[j, which, TOK:CHIP, :] = high[WINDOW:SPAN]

        @pl.when(has_far)
        def _():
            far_copy(j).start()

        swap(j)

        @pl.when(j == 1)
        def _():
            for n in range(2):
                relay(n + 2)
                pass_on(n)

        @pl.when(j == KVH - 1)
        def _():
            pass_on(KVH - 2)
            pass_on(KVH - 1)

    @pl.when(has_ahead)
    def _():
        wait(seg.at[2:4], seg_send)

    @pl.when(has_behind & has_ahead)
    def _():
        wait(seg.at[2:4], seg_relay_send)

    wait(seg.at[REACH], seg_swap_send)
    for n, (_, dst, _) in enumerate(swaps):
        wait(dst, swap_send.at[n])

    @pl.loop(0, KVH)
    def _(j):
        width = GROUP * DIM
        @pl.when(has_ahead)
        def _():
            wait(head_rows(CHIP, j), own_send.at[j])

        @pl.when(has_behind & has_ahead)
        def _():
            wait(head_rows(0, j), relay_send.at[j])

        @pl.when(has_far)
        def _():
            wait(far_out.at[j], far_send.at[j])

        @pl.when(has_behind)
        def _():
            wait(near_out.at[j], near_send.at[j])

        wait(dq.at[0:TOK, lanes(j * width, width)], dq_send.at[j])
        wait(dq.at[:, lanes(j * width, width)], dq_recv.at[j])
        wait(own_out.at[j, :, 0:TOK, :], part_send.at[j])
        wait(own_out.at[j], part_recv.at[j])

        @pl.when(has_ahead)
        def _():
            for core in range(2):
                wait(
                    near_in.at[:, :, lanes(core * KVW + j * DIM, DIM)],
                    near_recv.at[core * KVH + j],
                )


def finish(dq_in, near_in, own_in, dq_hbm, dk_hbm, dv_hbm, grads, sems):
    dq_copy = pltpu.make_async_copy(dq_in, dq_hbm, sems.at[2])
    dq_copy.start()
    copies = [
        pltpu.make_async_copy(grads.at[n], out, sems.at[n])
        for n, out in enumerate((dk_hbm, dv_hbm))
    ]
    for n in range(2):
        grads[n] = (own_in[n] + near_in[n].astype(jnp.float32)).astype(grads.dtype)
        copies[n].start()
    for copy in (dq_copy, *copies):
        copy.wait()


def local(chips, fsdp, queries, keys, values, grad_out, segment):
    low = jnp.bfloat16
    dma = pltpu.SemaphoreType.DMA
    anywhere = pl.BlockSpec(memory_space=pl.ANY)
    inside = pl.BlockSpec(memory_space=pltpu.VMEM)
    pair = (2, TOK, 2 * KVW)
    parts = pl.pallas_call(
        functools.partial(kernel, chips, fsdp),
        out_shape=(
            pltpu.VMEM((TOK, 2 * QW), low),
            pltpu.VMEM(pair, low),
            pltpu.VMEM(pair, jnp.float32),
        ),
        in_specs=[anywhere] * 5,
        out_specs=(inside,) * 3,
        scratch_shapes=[
            pltpu.VMEM((2, ROWS, KVW), low),
            pltpu.VMEM((CHIP, QW), low),
            pltpu.VMEM((CHIP, QW), low),
            pltpu.VMEM((6, 1, TOK), jnp.int32),
            pltpu.VMEM((2, SPAN, TOK), jnp.float32),
            pltpu.VMEM((KVH, 2, CHIP, DIM), jnp.float32),
            pltpu.VMEM((KVH, 2, CHIP, DIM), jnp.float32),
            pltpu.VMEM((KVH, 2, CHIP, DIM), low),
            pltpu.VMEM((KVH, 2, CHIP, DIM), low),
            pltpu.VMEM((KVH, 2, CHIP, DIM), low),
            pltpu.VMEM((CHIP, QW), low),
            dma((KVH,)),
            dma((KVH,)),
            dma((KVH,)),
            dma((KVH,)),
            dma((4,)),
            dma((4,)),
            dma(()),
            dma(()),
            dma(()),
            dma(()),
            dma(()),
            dma(()),
            dma((KVH,)),
            dma((KVH,)),
            dma((KVH,)),
            dma((2 * KVH,)),
            dma((KVH,)),
            dma((KVH,)),
            dma((KVH,)),
            dma((KVH,)),
            pltpu.SemaphoreType.REGULAR,
        ],
        compiler_params=pltpu.CompilerParams(collective_id=0, has_side_effects=True),
        name="window_grads",
    )(queries, keys, values, grad_out, segment.reshape(1, TOK))
    return pl.pallas_call(
        finish,
        out_shape=tuple(jax.ShapeDtypeStruct(a.shape, low) for a in (queries, keys, values)),
        in_specs=[inside] * 3,
        out_specs=(anywhere,) * 3,
        scratch_shapes=[pltpu.VMEM(pair, low), dma((3,))],
        name="window_grads_out",
    )(*(pltpu.with_memory_space_constraint(part, pltpu.VMEM) for part in parts))


def solution(mesh):
    fsdp = mesh.shape["fsdp"]
    chips = mesh.shape["ctx"] * fsdp // 2
    split = P(("ctx", "fsdp"), None)
    return jax.shard_map(
        functools.partial(local, chips, fsdp),
        mesh=mesh,
        in_specs=(split, split, split, split, P(("ctx", "fsdp"))),
        out_specs=(split, split, split),
        check_vma=False,
    )
```

```python
import functools

import jax
import jax.numpy as jnp
from jax import lax
from jax.experimental import pallas as pl
from jax.experimental.pallas import tpu as pltpu
from jax.sharding import PartitionSpec as P

TOK = 128
DIM = 128
WINDOW = 512
KVH = 4
GROUP = 2
KVW = KVH * DIM
QW = KVW * GROUP
CHIP = 2 * TOK
REACH = WINDOW // TOK
ROWS = WINDOW + CHIP
SPAN = WINDOW + TOK
CAP = 50.0
SCALE = 1.0 / 12.0

NT = (((1,), (1,)), ((), ()))
NN = (((1,), (0,)), ((), ()))
TN = (((0,), (0,)), ((), ()))


def mm(lhs, rhs, dims):
    return lax.dot_general(lhs, rhs, dims, preferred_element_type=jnp.float32)


def kernel(
    chips,
    fsdp,
    q_hbm,
    k_hbm,
    v_hbm,
    do_hbm,
    seg_hbm,
    dq_out,
    near_in,
    own_in,
    kv,
    q,
    do,
    seg,
    mask,
    part,
    own_out,
    far_out,
    far_in,
    near_out,
    dq,
    own_send,
    own_recv,
    relay_send,
    relay_recv,
    swap_send,
    swap_recv,
    seg_send,
    seg_recv,
    seg_swap_send,
    seg_swap_recv,
    seg_relay_send,
    seg_relay_recv,
    far_send,
    far_recv,
    near_send,
    near_recv,
    dq_send,
    dq_recv,
    part_send,
    part_recv,
    ready,
):
    index = lax.axis_index("ctx") * fsdp + lax.axis_index("fsdp")
    chip = index // 2
    me = index % 2
    other = 1 - me

    def device(which_chip, core):
        at = which_chip * 2 + core
        return (at // fsdp, at % fsdp)

    ahead = (chip + 1) % chips
    behind = (chip + chips - 1) % chips
    partner = device(chip, other)

    def remote(src, dst, send, recv, to):
        return pltpu.make_async_remote_copy(
            src_ref=src,
            dst_ref=dst,
            send_sem=send,
            recv_sem=recv,
            device_id=to,
            device_id_type=pl.DeviceIdType.MESH,
        )

    def wait(ref, sem):
        pltpu.make_async_copy(ref, ref, sem).wait()

    def lanes(start, size):
        return pl.ds(pl.multiple_of(start, DIM), size)

    def rows(core, base=0):
        return pl.ds(pl.multiple_of(base + core * TOK, TOK), TOK)

    has_ahead = chip < chips - 1
    has_behind = chip > 0
    has_far = chip > 1

    def signal(sem, to):
        pl.semaphore_signal(sem, inc=1, device_id=to, device_id_type=pl.DeviceIdType.MESH)

    barrier = pltpu.get_barrier_semaphore()
    signal(barrier, partner)

    @pl.when(has_behind)
    def _():
        signal(barrier, device(behind, 0))
        signal(barrier, device(behind, 1))

    pl.semaphore_wait(barrier, 1 + 2 * jnp.where(has_ahead, 1, 0))

    @pl.when(has_ahead)
    def _():
        signal(ready, device(ahead, 0))
        signal(ready, device(ahead, 1))

    def send_own(j):
        @pl.when(has_ahead)
        def _():
            for which, src in ((0, k_hbm), (1, v_hbm)):
                for core in range(2):
                    remote(
                        src.at[:, lanes(core * KVW + j * DIM, DIM)],
                        kv.at[which, rows(me, CHIP), lanes(j * DIM, DIM)],
                        own_send.at[which, j],
                        own_recv.at[which, j],
                        device(ahead, core),
                    ).start()

    def head_rows(which, start, j):
        return kv.at[which, start : start + CHIP, lanes(j * DIM, DIM)]

    def relay(j):
        for which in range(2):
            @pl.when(has_behind)
            def _():
                wait(head_rows(which, CHIP, j), own_recv.at[which, j])

            @pl.when(has_behind & has_ahead)
            def _():
                remote(
                    head_rows(which, CHIP, j),
                    head_rows(which, 0, j),
                    relay_send.at[which, j],
                    relay_recv.at[which, j],
                    device(ahead, me),
                ).start()

    @pl.when(has_ahead)
    def _():
        for core in range(2):
            remote(seg_hbm, seg.at[2 + me], seg_send, seg_recv, device(ahead, core)).start()

    send_own(0)
    send_own(1)

    @pl.when(chip <= 1)
    def _():
        send_own(2)
        send_own(3)

    remote(seg_hbm, seg.at[REACH + me], seg_swap_send, seg_swap_recv, partner).start()
    pltpu.make_async_copy(seg_hbm, seg.at[REACH + me], seg_swap_recv).start()
    swaps = (
        (k_hbm, kv.at[0, rows(me, WINDOW), :], KVW),
        (v_hbm, kv.at[1, rows(me, WINDOW), :], KVW),
        (q_hbm, q.at[rows(me), :], QW),
        (do_hbm, do.at[rows(me), :], QW),
    )
    for n, (src, dst, width) in enumerate(swaps):
        remote(
            src.at[:, lanes(other * width, width)],
            dst,
            swap_send.at[n],
            swap_recv.at[n],
            partner,
        ).start()
        pltpu.make_async_copy(
            src.at[:, lanes(me * width, width)], dst, swap_recv.at[n]
        ).start()

    @pl.when(chip <= 1)
    def _():
        kv[:, 0:CHIP, :] = jnp.zeros((2, CHIP, KVW), kv.dtype)
        seg[0:2] = jnp.zeros((2, 1, TOK), seg.dtype)

    @pl.when(chip == 0)
    def _():
        kv[:, CHIP:WINDOW, :] = jnp.zeros((2, CHIP, KVW), kv.dtype)
        seg[2:4] = jnp.zeros((2, 1, TOK), seg.dtype)

    @pl.when(chip == chips - 1)
    def _():
        far_in[...] = jnp.zeros(far_in.shape, far_in.dtype)
        near_in[...] = jnp.zeros(near_in.shape, near_in.dtype)

    @pl.when(has_behind)
    def _():
        wait(seg.at[2:4], seg_recv)

    @pl.when(has_behind & has_ahead)
    def _():
        remote(
            seg.at[2:4], seg.at[0:2], seg_relay_send, seg_relay_recv, device(ahead, me)
        ).start()

    relay(0)
    relay(1)

    @pl.when(chip <= 2)
    def _():
        relay(2)
        relay(3)

    @pl.when(chip > 1)
    def _():
        send_own(2)
        send_own(3)

    wait(seg.at[4:6], seg_swap_recv)

    @pl.when(has_far)
    def _():
        wait(seg.at[0:2], seg_relay_recv)

    @pl.when(has_behind)
    def _():
        pl.semaphore_wait(ready, 2)

    key_at = lax.broadcasted_iota(jnp.int32, (TOK, TOK), 0)
    query_at = lax.broadcasted_iota(jnp.int32, (TOK, TOK), 1)
    for b in range(6):
        wide = jnp.broadcast_to(seg[b].astype(jnp.float32), (TOK, TOK))
        key_seg = wide.T
        real = jnp.where(2 * chip - REACH + b >= 0, 1.0, 0.0)
        for s in range(2):
            distance = REACH + s - b
            if distance < 0 or distance > REACH:
                continue
            query_seg = jnp.broadcast_to(seg[REACH + s].astype(jnp.float32), (TOK, TOK))
            seen = jnp.where(key_seg == query_seg, real, 0.0)
            if distance == 0:
                seen = jnp.where(query_at >= key_at, seen, 0.0)
            if distance == REACH:
                seen = jnp.where(query_at < key_at, seen, 0.0)
            at = (b - s) * TOK
            mask[s, at : at + TOK, :] = seen

    wait(kv.at[0, WINDOW:ROWS, :], swap_recv.at[0])
    wait(kv.at[1, WINDOW:ROWS, :], swap_recv.at[1])
    wait(q, swap_recv.at[2])
    wait(do, swap_recv.at[3])

    def stacked(ref, j, s):
        return jnp.concatenate(
            [
                ref[s * TOK : (s + 1) * TOK, lanes((j * GROUP + r) * DIM, DIM)]
                for r in range(GROUP)
            ],
            axis=0,
        )

    def key_rows(which, j, s):
        return kv[which, s * TOK : s * TOK + SPAN, lanes(j * DIM, DIM)]

    def forward(j, s):
        grads = stacked(do, j, s)
        seen = jnp.concatenate([mask[s]] * GROUP, axis=1)
        t = jnp.tanh(mm(key_rows(0, j, s), stacked(q, j, s), NT) * (SCALE / CAP))
        weights = jnp.exp(CAP * t) * seen
        total = jnp.sum(weights, axis=0, keepdims=True)
        probs = weights * (1.0 / total)
        probs_low = probs.astype(jnp.bfloat16)
        dprobs = mm(key_rows(1, j, s), grads, NT)
        return t, probs, probs_low, dprobs, mm(probs_low, grads, NN)

    def backward(j, s, t, probs, probs_low, dprobs):
        row_term = jnp.sum(probs_low.astype(jnp.float32) * dprobs, axis=0, keepdims=True)
        dscore = probs * (dprobs - row_term) * ((1.0 - t * t) * SCALE)
        dscore_low = dscore.astype(jnp.bfloat16)
        grad_q = mm(key_rows(0, j, s), dscore_low, TN).T
        for r in range(GROUP):
            dq[s * TOK : (s + 1) * TOK, lanes((j * GROUP + r) * DIM, DIM)] = grad_q[
                r * TOK : (r + 1) * TOK
            ].astype(jnp.bfloat16)
        return mm(dscore_low, stacked(q, j, s), NN)

    def far_copy(which, j):
        return remote(
            far_out.at[j, which],
            far_in.at[j, which],
            far_send.at[which, j],
            far_recv.at[which, j],
            device(behind, me),
        )

    def hand_out(which, j, low, high):
        far_out[j, which, 0:TOK, :] = low[0:TOK].astype(jnp.bfloat16)
        far_out[j, which, TOK:CHIP, :] = (low[TOK:CHIP] + high[0:TOK]).astype(jnp.bfloat16)

        @pl.when(has_far)
        def _():
            far_copy(which, j).start()

        part[j, which] = low[CHIP:WINDOW] + high[TOK : WINDOW - TOK]
        own_out[j, which, 0:TOK, :] = low[WINDOW:SPAN] + high[WINDOW - TOK : WINDOW]
        own_out[j, which, TOK:CHIP, :] = high[WINDOW:SPAN]

    def send_near(which, j):
        for core in range(2):
            remote(
                near_out.at[j, which, core * TOK : (core + 1) * TOK, :],
                near_in.at[which, :, lanes(me * KVW + j * DIM, DIM)],
                near_send.at[which, j],
                near_recv.at[which, me * KVH + j],
                device(behind, core),
            ).start()

    def pass_on(j):
        @pl.when(has_behind)
        def _():
            for which in (1, 0):
                @pl.when(has_ahead)
                def _():
                    wait(far_in.at[j, which], far_recv.at[which, j])

                near_out[j, which] = (
                    part[j, which] + far_in[j, which].astype(jnp.float32)
                ).astype(jnp.bfloat16)
                send_near(which, j)

    def swap(j):
        width = GROUP * DIM
        into = lanes(me * QW + j * width, width)
        cols = lanes(j * width, width)
        remote(
            dq.at[rows(other), cols], dq_out.at[:, into], dq_send.at[j], dq_recv.at[j], partner
        ).start()
        pltpu.make_async_copy(dq.at[rows(me), cols], dq_out.at[:, into], dq_recv.at[j]).start()
        into = lanes(me * KVW + j * DIM, DIM)
        remote(
            own_out.at[j, :, rows(other), :],
            own_in.at[:, :, into],
            part_send.at[j],
            part_recv.at[j],
            partner,
        ).start()
        pltpu.make_async_copy(
            own_out.at[j, :, rows(me), :], own_in.at[:, :, into], part_recv.at[j]
        ).start()

    @pl.loop(0, KVH)
    def _(j):
        @pl.when(has_far)
        def _():
            for which in range(2):
                wait(head_rows(which, 0, j), relay_recv.at[which, j])

        *first, low = forward(j, 0)
        *second, high = forward(j, 1)
        hand_out(1, j, low, high)
        hand_out(0, j, backward(j, 0, *first), backward(j, 1, *second))

        swap(j)

        @pl.when(j == 1)
        def _():
            for n in range(2):
                @pl.when(chip > 2)
                def _():
                    relay(n + 2)

                @pl.when(chip != 2)
                def _():
                    pass_on(n)

        @pl.when(j == KVH - 1)
        def _():
            @pl.when(chip == 2)
            def _():
                pass_on(0)
                pass_on(1)

            pass_on(2)
            pass_on(3)

    @pl.when(has_ahead)
    def _():
        wait(seg.at[2:4], seg_send)

    @pl.when(has_behind & has_ahead)
    def _():
        wait(seg.at[2:4], seg_relay_send)

    wait(seg.at[REACH], seg_swap_send)
    for n, (_, dst, _) in enumerate(swaps):
        wait(dst, swap_send.at[n])

    @pl.loop(0, KVH)
    def _(j):
        width = GROUP * DIM
        for which in range(2):
            @pl.when(has_ahead)
            def _():
                wait(head_rows(which, CHIP, j), own_send.at[which, j])

            @pl.when(has_behind & has_ahead)
            def _():
                wait(head_rows(which, 0, j), relay_send.at[which, j])

            @pl.when(has_far)
            def _():
                wait(far_out.at[j, which], far_send.at[which, j])

            @pl.when(has_behind)
            def _():
                wait(near_out.at[j, which], near_send.at[which, j])

        wait(dq.at[0:TOK, lanes(j * width, width)], dq_send.at[j])
        wait(dq.at[:, lanes(j * width, width)], dq_recv.at[j])
        wait(own_out.at[j, :, 0:TOK, :], part_send.at[j])
        wait(own_out.at[j], part_recv.at[j])

        @pl.when(has_ahead)
        def _():
            for which in range(2):
                for core in range(2):
                    wait(
                        near_in.at[which, :, lanes(core * KVW + j * DIM, DIM)],
                        near_recv.at[which, core * KVH + j],
                    )


def finish(dq_in, near_in, own_in, dq_hbm, dk_hbm, dv_hbm, grads, sems):
    dq_copy = pltpu.make_async_copy(dq_in, dq_hbm, sems.at[2])
    dq_copy.start()
    copies = [
        pltpu.make_async_copy(grads.at[n], out, sems.at[n])
        for n, out in enumerate((dk_hbm, dv_hbm))
    ]
    for n in range(2):
        grads[n] = (own_in[n] + near_in[n].astype(jnp.float32)).astype(grads.dtype)
        copies[n].start()
    for copy in (dq_copy, *copies):
        copy.wait()


def local(chips, fsdp, queries, keys, values, grad_out, segment):
    low = jnp.bfloat16
    dma = pltpu.SemaphoreType.DMA
    anywhere = pl.BlockSpec(memory_space=pl.ANY)
    inside = pl.BlockSpec(memory_space=pltpu.VMEM)
    pair = (2, TOK, 2 * KVW)
    parts = pl.pallas_call(
        functools.partial(kernel, chips, fsdp),
        out_shape=(
            pltpu.VMEM((TOK, 2 * QW), low),
            pltpu.VMEM(pair, low),
            pltpu.VMEM(pair, jnp.float32),
        ),
        in_specs=[anywhere] * 5,
        out_specs=(inside,) * 3,
        scratch_shapes=[
            pltpu.VMEM((2, ROWS, KVW), low),
            pltpu.VMEM((CHIP, QW), low),
            pltpu.VMEM((CHIP, QW), low),
            pltpu.VMEM((6, 1, TOK), jnp.int32),
            pltpu.VMEM((2, SPAN, TOK), jnp.float32),
            pltpu.VMEM((KVH, 2, CHIP, DIM), jnp.float32),
            pltpu.VMEM((KVH, 2, CHIP, DIM), jnp.float32),
            pltpu.VMEM((KVH, 2, CHIP, DIM), low),
            pltpu.VMEM((KVH, 2, CHIP, DIM), low),
            pltpu.VMEM((KVH, 2, CHIP, DIM), low),
            pltpu.VMEM((CHIP, QW), low),
            dma((2, KVH)),
            dma((2, KVH)),
            dma((2, KVH)),
            dma((2, KVH)),
            dma((4,)),
            dma((4,)),
            dma(()),
            dma(()),
            dma(()),
            dma(()),
            dma(()),
            dma(()),
            dma((2, KVH)),
            dma((2, KVH)),
            dma((2, KVH)),
            dma((2, 2 * KVH)),
            dma((KVH,)),
            dma((KVH,)),
            dma((KVH,)),
            dma((KVH,)),
            pltpu.SemaphoreType.REGULAR,
        ],
        compiler_params=pltpu.CompilerParams(collective_id=0, has_side_effects=True),
        name="window_grads",
    )(queries, keys, values, grad_out, segment.reshape(1, TOK))
    return pl.pallas_call(
        finish,
        out_shape=tuple(jax.ShapeDtypeStruct(a.shape, low) for a in (queries, keys, values)),
        in_specs=[inside] * 3,
        out_specs=(anywhere,) * 3,
        scratch_shapes=[pltpu.VMEM(pair, low), dma((3,))],
        name="window_grads_out",
    )(*(pltpu.with_memory_space_constraint(part, pltpu.VMEM) for part in parts))


def solution(mesh):
    fsdp = mesh.shape["fsdp"]
    chips = mesh.shape["ctx"] * fsdp // 2
    split = P(("ctx", "fsdp"), None)
    return jax.shard_map(
        functools.partial(local, chips, fsdp),
        mesh=mesh,
        in_specs=(split, split, split, split, P(("ctx", "fsdp"))),
        out_specs=(split, split, split),
        check_vma=False,
    )
```

```python
import functools

import jax
import jax.numpy as jnp
from jax import lax
from jax.experimental import pallas as pl
from jax.experimental.pallas import tpu as pltpu
from jax.sharding import PartitionSpec as P

TOK = 128
DIM = 128
WINDOW = 512
KVH = 4
GROUP = 2
KVW = KVH * DIM
QW = KVW * GROUP
CHIP = 2 * TOK
REACH = WINDOW // TOK
ROWS = WINDOW + CHIP
SPAN = WINDOW + TOK
CAP = 50.0
SCALE = 1.0 / 12.0

NT = (((1,), (1,)), ((), ()))
NN = (((1,), (0,)), ((), ()))
TN = (((0,), (0,)), ((), ()))


def mm(lhs, rhs, dims):
    return lax.dot_general(lhs, rhs, dims, preferred_element_type=jnp.float32)


def kernel(
    chips,
    fsdp,
    q_hbm,
    k_hbm,
    v_hbm,
    do_hbm,
    seg_hbm,
    dq_out,
    near_in,
    own_in,
    kv,
    q,
    do,
    seg,
    mask,
    part,
    own_out,
    far_out,
    far_in,
    near_out,
    dq,
    own_send,
    own_recv,
    relay_send,
    relay_recv,
    swap_send,
    swap_recv,
    seg_send,
    seg_recv,
    seg_swap_send,
    seg_swap_recv,
    seg_relay_send,
    seg_relay_recv,
    far_send,
    far_recv,
    near_send,
    near_recv,
    dq_send,
    dq_recv,
    part_send,
    part_recv,
    ready,
):
    row, column = lax.axis_index("ctx"), lax.axis_index("fsdp")
    me = column % 2
    other = 1 - me
    start = column - me
    row_chips = fsdp // 2
    chip = row * row_chips + start // 2
    partner = (row, start + other)
    rows_all = chips // row_chips
    turns, turned = start == fsdp - 2, start == 0
    ahead = (
        jnp.where(turns, jnp.where(row == rows_all - 1, 0, row + 1), row),
        jnp.where(turns, 0, start + 2),
    )
    behind = (
        jnp.where(turned, jnp.where(row == 0, rows_all - 1, row - 1), row),
        jnp.where(turned, fsdp - 2, start - 2),
    )

    def device(at, core):
        return (at[0], at[1] + core)

    def remote(src, dst, send, recv, to):
        return pltpu.make_async_remote_copy(
            src_ref=src,
            dst_ref=dst,
            send_sem=send,
            recv_sem=recv,
            device_id=to,
            device_id_type=pl.DeviceIdType.MESH,
        )

    def wait(ref, sem):
        pltpu.make_async_copy(ref, ref, sem).wait()

    def lanes(start, size):
        return pl.ds(pl.multiple_of(start, DIM), size)

    def rows(core, base=0):
        return pl.ds(pl.multiple_of(base + core * TOK, TOK), TOK)

    has_ahead = chip < chips - 1
    has_behind = chip > 0
    has_far = chip > 1

    def signal(sem, to):
        pl.semaphore_signal(sem, inc=1, device_id=to, device_id_type=pl.DeviceIdType.MESH)

    barrier = pltpu.get_barrier_semaphore()

    @pl.when(has_behind)
    def _():
        signal(barrier, device(behind, 0))
        signal(barrier, device(behind, 1))

    signal(barrier, partner)
    pl.semaphore_wait(barrier, 1 + 2 * jnp.where(has_ahead, 1, 0))

    @pl.when(has_ahead)
    def _():
        signal(ready, device(ahead, 0))
        signal(ready, device(ahead, 1))

    def send_own(j):
        @pl.when(has_ahead)
        def _():
            for which, src in ((0, k_hbm), (1, v_hbm)):
                for core in range(2):
                    remote(
                        src.at[:, lanes(core * KVW + j * DIM, DIM)],
                        kv.at[which, rows(me, CHIP), lanes(j * DIM, DIM)],
                        own_send.at[which, j],
                        own_recv.at[which, j],
                        device(ahead, core),
                    ).start()

    def head_rows(which, start, j):
        return kv.at[which, start : start + CHIP, lanes(j * DIM, DIM)]

    def relay(j):
        for which in range(2):
            @pl.when(has_behind)
            def _():
                wait(head_rows(which, CHIP, j), own_recv.at[which, j])

            @pl.when(has_behind & has_ahead)
            def _():
                remote(
                    head_rows(which, CHIP, j),
                    head_rows(which, 0, j),
                    relay_send.at[which, j],
                    relay_recv.at[which, j],
                    device(ahead, me),
                ).start()

    @pl.when(has_ahead)
    def _():
        for core in range(2):
            remote(seg_hbm, seg.at[2 + me], seg_send, seg_recv, device(ahead, core)).start()

    send_own(0)
    send_own(1)

    @pl.when(chip <= 1)
    def _():
        send_own(2)
        send_own(3)

    remote(seg_hbm, seg.at[REACH + me], seg_swap_send, seg_swap_recv, partner).start()
    pltpu.make_async_copy(seg_hbm, seg.at[REACH + me], seg_swap_recv).start()
    swaps = (
        (k_hbm, kv.at[0, rows(me, WINDOW), :], KVW),
        (v_hbm, kv.at[1, rows(me, WINDOW), :], KVW),
        (q_hbm, q.at[rows(me), :], QW),
        (do_hbm, do.at[rows(me), :], QW),
    )
    for n, (src, dst, width) in enumerate(swaps):
        remote(
            src.at[:, lanes(other * width, width)],
            dst,
            swap_send.at[n],
            swap_recv.at[n],
            partner,
        ).start()
        pltpu.make_async_copy(
            src.at[:, lanes(me * width, width)], dst, swap_recv.at[n]
        ).start()

    @pl.when(chip <= 1)
    def _():
        kv[:, 0:CHIP, :] = jnp.zeros((2, CHIP, KVW), kv.dtype)
        seg[0:2] = jnp.zeros((2, 1, TOK), seg.dtype)

    @pl.when(chip == 0)
    def _():
        kv[:, CHIP:WINDOW, :] = jnp.zeros((2, CHIP, KVW), kv.dtype)
        seg[2:4] = jnp.zeros((2, 1, TOK), seg.dtype)

    @pl.when(chip == chips - 1)
    def _():
        far_in[...] = jnp.zeros(far_in.shape, far_in.dtype)
        near_in[...] = jnp.zeros(near_in.shape, near_in.dtype)

    @pl.when(has_behind)
    def _():
        wait(seg.at[2:4], seg_recv)

    @pl.when(has_behind & has_ahead)
    def _():
        remote(
            seg.at[2:4], seg.at[0:2], seg_relay_send, seg_relay_recv, device(ahead, me)
        ).start()

    relay(0)
    relay(1)

    @pl.when(chip <= 2)
    def _():
        relay(2)
        relay(3)

    @pl.when(chip > 1)
    def _():
        send_own(2)
        send_own(3)

    wait(seg.at[4:6], seg_swap_recv)

    @pl.when(has_far)
    def _():
        wait(seg.at[0:2], seg_relay_recv)

    @pl.when(has_behind)
    def _():
        pl.semaphore_wait(ready, 2)

    key_at = lax.broadcasted_iota(jnp.int32, (TOK, TOK), 0)
    query_at = lax.broadcasted_iota(jnp.int32, (TOK, TOK), 1)
    for b in range(6):
        wide = jnp.broadcast_to(seg[b].astype(jnp.float32), (TOK, TOK))
        key_seg = wide.T
        real = jnp.where(2 * chip - REACH + b >= 0, 1.0, 0.0)
        for s in range(2):
            distance = REACH + s - b
            if distance < 0 or distance > REACH:
                continue
            query_seg = jnp.broadcast_to(seg[REACH + s].astype(jnp.float32), (TOK, TOK))
            seen = jnp.where(key_seg == query_seg, real, 0.0)
            if distance == 0:
                seen = jnp.where(query_at >= key_at, seen, 0.0)
            if distance == REACH:
                seen = jnp.where(query_at < key_at, seen, 0.0)
            at = (b - s) * TOK
            mask[s, at : at + TOK, :] = seen

    wait(kv.at[0, WINDOW:ROWS, :], swap_recv.at[0])
    wait(kv.at[1, WINDOW:ROWS, :], swap_recv.at[1])
    wait(q, swap_recv.at[2])
    wait(do, swap_recv.at[3])

    def stacked(ref, j, s):
        return jnp.concatenate(
            [
                ref[s * TOK : (s + 1) * TOK, lanes((j * GROUP + r) * DIM, DIM)]
                for r in range(GROUP)
            ],
            axis=0,
        )

    def scores(j, s, queries, grads, low, high):
        keys = kv[0, low:high, lanes(j * DIM, DIM)]
        vals = kv[1, low:high, lanes(j * DIM, DIM)]
        seen = jnp.concatenate([mask[s, low - s * TOK : high - s * TOK]] * GROUP, axis=1)
        t = jnp.tanh(mm(keys, queries, NT) * (SCALE / CAP))
        return t, jnp.exp(CAP * t) * seen, mm(vals, grads, NT)

    def column_sum(a):
        return jnp.sum(a, axis=0, keepdims=True)

    def score_grads(t, probs, dprobs, row_term):
        dscore = probs * (dprobs - row_term) * ((1.0 - t * t) * SCALE)
        return dscore.astype(jnp.bfloat16)

    def far_copy(which, j):
        return remote(
            far_out.at[j, which],
            far_in.at[j, which],
            far_send.at[which, j],
            far_recv.at[which, j],
            device(behind, me),
        )

    def far_out_of(which, j, low, high):
        far_out[j, which, 0:TOK, :] = low[0:TOK].astype(jnp.bfloat16)
        far_out[j, which, TOK:CHIP, :] = (low[TOK:CHIP] + high).astype(jnp.bfloat16)

        @pl.when(has_far)
        def _():
            far_copy(which, j).start()

    def rest_of(which, j, low, high):
        part[j, which] = low[0:CHIP] + high[0:CHIP]
        own_out[j, which, 0:TOK, :] = low[CHIP : CHIP + TOK] + high[CHIP : CHIP + TOK]
        own_out[j, which, TOK:CHIP, :] = high[CHIP + TOK : WINDOW]

    def send_near(which, j):
        for core in range(2):
            remote(
                near_out.at[j, which, core * TOK : (core + 1) * TOK, :],
                near_in.at[which, :, lanes(me * KVW + j * DIM, DIM)],
                near_send.at[which, j],
                near_recv.at[which, me * KVH + j],
                device(behind, core),
            ).start()

    def pass_on(j):
        @pl.when(has_behind)
        def _():
            for which in (1, 0):
                @pl.when(has_ahead)
                def _():
                    wait(far_in.at[j, which], far_recv.at[which, j])

                near_out[j, which] = (
                    part[j, which] + far_in[j, which].astype(jnp.float32)
                ).astype(jnp.bfloat16)
                send_near(which, j)

    def swap(j):
        width = GROUP * DIM
        into = lanes(me * QW + j * width, width)
        cols = lanes(j * width, width)
        remote(
            dq.at[rows(other), cols], dq_out.at[:, into], dq_send.at[j], dq_recv.at[j], partner
        ).start()
        pltpu.make_async_copy(dq.at[rows(me), cols], dq_out.at[:, into], dq_recv.at[j]).start()
        into = lanes(me * KVW + j * DIM, DIM)
        remote(
            own_out.at[j, :, rows(other), :],
            own_in.at[:, :, into],
            part_send.at[j],
            part_recv.at[j],
            partner,
        ).start()
        pltpu.make_async_copy(
            own_out.at[j, :, rows(me), :], own_in.at[:, :, into], part_recv.at[j]
        ).start()

    @pl.loop(0, KVH)
    def _(j):
        queries = [stacked(q, j, s) for s in range(2)]
        grads = [stacked(do, j, s) for s in range(2)]

        near = [scores(j, s, queries[s], grads[s], CHIP, s * TOK + SPAN) for s in range(2)]

        @pl.when(has_far)
        def _():
            for which in range(2):
                wait(head_rows(which, 0, j), relay_recv.at[which, j])

        far = [scores(j, s, queries[s], grads[s], s * TOK, CHIP) for s in range(2)]
        probs = []
        for s in range(2):
            inverse = 1.0 / (column_sum(far[s][1]) + column_sum(near[s][1]))
            probs.append((far[s][1] * inverse, near[s][1] * inverse))
        low = [[p.astype(jnp.bfloat16) for p in pair] for pair in probs]
        far_out_of(1, j, *(mm(low[s][0], grads[s], NN) for s in range(2)))

        far_low, row_terms = [], []
        for s in range(2):
            row_terms.append(
                column_sum(low[s][0].astype(jnp.float32) * far[s][2])
                + column_sum(low[s][1].astype(jnp.float32) * near[s][2])
            )
            far_low.append(score_grads(far[s][0], probs[s][0], far[s][2], row_terms[s]))
        far_out_of(0, j, *(mm(far_low[s], queries[s], NN) for s in range(2)))

        near_low = [
            score_grads(near[s][0], probs[s][1], near[s][2], row_terms[s]) for s in range(2)
        ]
        rest_of(1, j, *(mm(low[s][1], grads[s], NN) for s in range(2)))
        rest_of(0, j, *(mm(near_low[s], queries[s], NN) for s in range(2)))
        for s in range(2):
            keys = kv[0, s * TOK : s * TOK + SPAN, lanes(j * DIM, DIM)]
            both = jnp.concatenate([far_low[s], near_low[s]], axis=0)
            grad_q = mm(keys, both, TN).T
            for r in range(GROUP):
                dq[s * TOK : (s + 1) * TOK, lanes((j * GROUP + r) * DIM, DIM)] = grad_q[
                    r * TOK : (r + 1) * TOK
                ].astype(jnp.bfloat16)

        swap(j)

        @pl.when(j == 1)
        def _():
            for n in range(2):
                @pl.when(chip > 2)
                def _():
                    relay(n + 2)

                @pl.when(chip != 2)
                def _():
                    pass_on(n)

        @pl.when(j == KVH - 1)
        def _():
            @pl.when(chip == 2)
            def _():
                pass_on(0)
                pass_on(1)

            pass_on(2)
            pass_on(3)

    @pl.when(has_ahead)
    def _():
        wait(seg.at[2:4], seg_send)

    @pl.when(has_behind & has_ahead)
    def _():
        wait(seg.at[2:4], seg_relay_send)

    wait(seg.at[REACH], seg_swap_send)
    for n, (_, dst, _) in enumerate(swaps):
        wait(dst, swap_send.at[n])

    @pl.loop(0, KVH)
    def _(j):
        width = GROUP * DIM
        for which in range(2):
            @pl.when(has_ahead)
            def _():
                wait(head_rows(which, CHIP, j), own_send.at[which, j])

            @pl.when(has_behind & has_ahead)
            def _():
                wait(head_rows(which, 0, j), relay_send.at[which, j])

            @pl.when(has_far)
            def _():
                wait(far_out.at[j, which], far_send.at[which, j])

            @pl.when(has_behind)
            def _():
                wait(near_out.at[j, which], near_send.at[which, j])

        wait(dq.at[0:TOK, lanes(j * width, width)], dq_send.at[j])
        wait(dq.at[:, lanes(j * width, width)], dq_recv.at[j])
        wait(own_out.at[j, :, 0:TOK, :], part_send.at[j])
        wait(own_out.at[j], part_recv.at[j])

        @pl.when(has_ahead)
        def _():
            for which in range(2):
                for core in range(2):
                    wait(
                        near_in.at[which, :, lanes(core * KVW + j * DIM, DIM)],
                        near_recv.at[which, core * KVH + j],
                    )


def finish(dq_in, near_in, own_in, dq_hbm, dk_hbm, dv_hbm, grads, sems):
    dq_copy = pltpu.make_async_copy(dq_in, dq_hbm, sems.at[2])
    dq_copy.start()
    copies = [
        pltpu.make_async_copy(grads.at[n], out, sems.at[n])
        for n, out in enumerate((dk_hbm, dv_hbm))
    ]
    for n in range(2):
        grads[n] = (own_in[n] + near_in[n].astype(jnp.float32)).astype(grads.dtype)
        copies[n].start()
    for copy in (dq_copy, *copies):
        copy.wait()


def local(chips, fsdp, queries, keys, values, grad_out, segment):
    low = jnp.bfloat16
    dma = pltpu.SemaphoreType.DMA
    anywhere = pl.BlockSpec(memory_space=pl.ANY)
    inside = pl.BlockSpec(memory_space=pltpu.VMEM)
    pair = (2, TOK, 2 * KVW)
    parts = pl.pallas_call(
        functools.partial(kernel, chips, fsdp),
        out_shape=(
            pltpu.VMEM((TOK, 2 * QW), low),
            pltpu.VMEM(pair, low),
            pltpu.VMEM(pair, jnp.float32),
        ),
        in_specs=[anywhere] * 5,
        out_specs=(inside,) * 3,
        scratch_shapes=[
            pltpu.VMEM((2, ROWS, KVW), low),
            pltpu.VMEM((CHIP, QW), low),
            pltpu.VMEM((CHIP, QW), low),
            pltpu.VMEM((6, 1, TOK), jnp.int32),
            pltpu.VMEM((2, SPAN, TOK), jnp.float32),
            pltpu.VMEM((KVH, 2, CHIP, DIM), jnp.float32),
            pltpu.VMEM((KVH, 2, CHIP, DIM), jnp.float32),
            pltpu.VMEM((KVH, 2, CHIP, DIM), low),
            pltpu.VMEM((KVH, 2, CHIP, DIM), low),
            pltpu.VMEM((KVH, 2, CHIP, DIM), low),
            pltpu.VMEM((CHIP, QW), low),
            dma((2, KVH)),
            dma((2, KVH)),
            dma((2, KVH)),
            dma((2, KVH)),
            dma((4,)),
            dma((4,)),
            dma(()),
            dma(()),
            dma(()),
            dma(()),
            dma(()),
            dma(()),
            dma((2, KVH)),
            dma((2, KVH)),
            dma((2, KVH)),
            dma((2, 2 * KVH)),
            dma((KVH,)),
            dma((KVH,)),
            dma((KVH,)),
            dma((KVH,)),
            pltpu.SemaphoreType.REGULAR,
        ],
        compiler_params=pltpu.CompilerParams(collective_id=0, has_side_effects=True),
        name="window_grads",
    )(queries, keys, values, grad_out, segment.reshape(1, TOK))
    return pl.pallas_call(
        finish,
        out_shape=tuple(jax.ShapeDtypeStruct(a.shape, low) for a in (queries, keys, values)),
        in_specs=[inside] * 3,
        out_specs=(anywhere,) * 3,
        scratch_shapes=[pltpu.VMEM(pair, low), dma((3,))],
        name="window_grads_out",
    )(*(pltpu.with_memory_space_constraint(part, pltpu.VMEM) for part in parts))


def solution(mesh):
    fsdp = mesh.shape["fsdp"]
    chips = mesh.shape["ctx"] * fsdp // 2
    split = P(("ctx", "fsdp"), None)
    return jax.shard_map(
        functools.partial(local, chips, fsdp),
        mesh=mesh,
        in_specs=(split, split, split, split, P(("ctx", "fsdp"))),
        out_specs=(split, split, split),
        check_vma=False,
    )
```

```python
import functools

import jax
import jax.numpy as jnp
from jax import lax
from jax.experimental import pallas as pl
from jax.experimental.pallas import tpu as pltpu
from jax.sharding import PartitionSpec as P

TOK = 128
DIM = 128
WINDOW = 512
KVH = 4
GROUP = 2
KVW = KVH * DIM
QW = KVW * GROUP
CHIP = 2 * TOK
REACH = WINDOW // TOK
ROWS = WINDOW + CHIP
SPAN = WINDOW + TOK
CAP = 50.0
SCALE = 1.0 / 12.0

NT = (((1,), (1,)), ((), ()))
NN = (((1,), (0,)), ((), ()))
TN = (((0,), (0,)), ((), ()))


def mm(lhs, rhs, dims):
    return lax.dot_general(lhs, rhs, dims, preferred_element_type=jnp.float32)


def kernel(
    chips,
    fsdp,
    q_hbm,
    k_hbm,
    v_hbm,
    do_hbm,
    seg_hbm,
    dq_out,
    near_in,
    own_in,
    kv,
    q,
    do,
    seg,
    mask,
    part,
    own_out,
    far_out,
    far_in,
    near_out,
    dq,
    own_send,
    own_recv,
    relay_send,
    relay_recv,
    swap_send,
    swap_recv,
    seg_send,
    seg_recv,
    seg_swap_send,
    seg_swap_recv,
    seg_relay_send,
    seg_relay_recv,
    far_send,
    far_recv,
    near_send,
    near_recv,
    dq_send,
    dq_recv,
    part_send,
    part_recv,
    ready,
):
    row, column = lax.axis_index("ctx"), lax.axis_index("fsdp")
    me = column % 2
    other = 1 - me
    start = column - me
    row_chips = fsdp // 2
    chip = row * row_chips + start // 2
    partner = (row, start + other)
    rows_all = chips // row_chips
    turns, turned = start == fsdp - 2, start == 0
    ahead = (
        jnp.where(turns, jnp.where(row == rows_all - 1, 0, row + 1), row),
        jnp.where(turns, 0, start + 2),
    )
    behind = (
        jnp.where(turned, jnp.where(row == 0, rows_all - 1, row - 1), row),
        jnp.where(turned, fsdp - 2, start - 2),
    )

    def device(at, core):
        return (at[0], at[1] + core)

    def remote(src, dst, send, recv, to):
        return pltpu.make_async_remote_copy(
            src_ref=src,
            dst_ref=dst,
            send_sem=send,
            recv_sem=recv,
            device_id=to,
            device_id_type=pl.DeviceIdType.MESH,
        )

    def wait(ref, sem):
        pltpu.make_async_copy(ref, ref, sem).wait()

    def lanes(start, size):
        return pl.ds(pl.multiple_of(start, DIM), size)

    def rows(core, base=0):
        return pl.ds(pl.multiple_of(base + core * TOK, TOK), TOK)

    has_ahead = chip < chips - 1
    has_behind = chip > 0
    has_far = chip > 1

    def signal(sem, to):
        pl.semaphore_signal(sem, inc=1, device_id=to, device_id_type=pl.DeviceIdType.MESH)

    barrier = pltpu.get_barrier_semaphore()

    @pl.when(has_behind)
    def _():
        signal(barrier, device(behind, 0))
        signal(barrier, device(behind, 1))

    signal(barrier, partner)
    pl.semaphore_wait(barrier, 1 + 2 * jnp.where(has_ahead, 1, 0))

    @pl.when(has_ahead)
    def _():
        signal(ready, device(ahead, 0))
        signal(ready, device(ahead, 1))

    def send_own(j):
        @pl.when(has_ahead)
        def _():
            for which, src in ((0, k_hbm), (1, v_hbm)):
                for core in range(2):
                    remote(
                        src.at[:, lanes(core * KVW + j * DIM, DIM)],
                        kv.at[which, rows(me, CHIP), lanes(j * DIM, DIM)],
                        own_send.at[which, j],
                        own_recv.at[which, j],
                        device(ahead, core),
                    ).start()

    def head_rows(which, start, j):
        return kv.at[which, start : start + CHIP, lanes(j * DIM, DIM)]

    def relay(j):
        for which in range(2):
            @pl.when(has_behind)
            def _():
                wait(head_rows(which, CHIP, j), own_recv.at[which, j])

            @pl.when(has_behind & has_ahead)
            def _():
                remote(
                    head_rows(which, CHIP, j),
                    head_rows(which, 0, j),
                    relay_send.at[which, j],
                    relay_recv.at[which, j],
                    device(ahead, me),
                ).start()

    @pl.when(has_ahead)
    def _():
        for core in range(2):
            remote(seg_hbm, seg.at[2 + me], seg_send, seg_recv, device(ahead, core)).start()

    send_own(0)
    send_own(1)

    @pl.when(chip <= 1)
    def _():
        send_own(2)
        send_own(3)

    remote(seg_hbm, seg.at[REACH + me], seg_swap_send, seg_swap_recv, partner).start()
    pltpu.make_async_copy(seg_hbm, seg.at[REACH + me], seg_swap_recv).start()
    swaps = (
        (k_hbm, kv.at[0, rows(me, WINDOW), :], KVW),
        (v_hbm, kv.at[1, rows(me, WINDOW), :], KVW),
        (q_hbm, q.at[rows(me), :], QW),
        (do_hbm, do.at[rows(me), :], QW),
    )
    for n, (src, dst, width) in enumerate(swaps):
        remote(
            src.at[:, lanes(other * width, width)],
            dst,
            swap_send.at[n],
            swap_recv.at[n],
            partner,
        ).start()
        pltpu.make_async_copy(
            src.at[:, lanes(me * width, width)], dst, swap_recv.at[n]
        ).start()

    @pl.when(chip <= 1)
    def _():
        kv[:, 0:CHIP, :] = jnp.zeros((2, CHIP, KVW), kv.dtype)
        seg[0:2] = jnp.zeros((2, 1, TOK), seg.dtype)

    @pl.when(chip == 0)
    def _():
        kv[:, CHIP:WINDOW, :] = jnp.zeros((2, CHIP, KVW), kv.dtype)
        seg[2:4] = jnp.zeros((2, 1, TOK), seg.dtype)

    @pl.when(chip == chips - 1)
    def _():
        far_in[...] = jnp.zeros(far_in.shape, far_in.dtype)
        near_in[...] = jnp.zeros(near_in.shape, near_in.dtype)

    @pl.when(has_behind)
    def _():
        wait(seg.at[2:4], seg_recv)

    @pl.when(has_behind & has_ahead)
    def _():
        remote(
            seg.at[2:4], seg.at[0:2], seg_relay_send, seg_relay_recv, device(ahead, me)
        ).start()

    relay(0)
    relay(1)

    @pl.when(chip > 1)
    def _():
        send_own(2)
        send_own(3)

    @pl.when(chip <= 2)
    def _():
        relay(2)
        relay(3)

    wait(seg.at[4:6], seg_swap_recv)

    @pl.when(has_far)
    def _():
        wait(seg.at[0:2], seg_relay_recv)

    @pl.when(has_behind)
    def _():
        pl.semaphore_wait(ready, 2)

    key_at = lax.broadcasted_iota(jnp.int32, (TOK, TOK), 0)
    query_at = lax.broadcasted_iota(jnp.int32, (TOK, TOK), 1)
    for b in range(6):
        wide = jnp.broadcast_to(seg[b].astype(jnp.float32), (TOK, TOK))
        key_seg = wide.T
        real = jnp.where(2 * chip - REACH + b >= 0, 1.0, 0.0)
        for s in range(2):
            distance = REACH + s - b
            if distance < 0 or distance > REACH:
                continue
            query_seg = jnp.broadcast_to(seg[REACH + s].astype(jnp.float32), (TOK, TOK))
            seen = jnp.where(key_seg == query_seg, real, 0.0)
            if distance == 0:
                seen = jnp.where(query_at >= key_at, seen, 0.0)
            if distance == REACH:
                seen = jnp.where(query_at < key_at, seen, 0.0)
            at = (b - s) * TOK
            mask[s, at : at + TOK, :] = seen

    wait(kv.at[0, WINDOW:ROWS, :], swap_recv.at[0])
    wait(kv.at[1, WINDOW:ROWS, :], swap_recv.at[1])
    wait(q, swap_recv.at[2])
    wait(do, swap_recv.at[3])

    def stacked(ref, j, s):
        return jnp.concatenate(
            [
                ref[s * TOK : (s + 1) * TOK, lanes((j * GROUP + r) * DIM, DIM)]
                for r in range(GROUP)
            ],
            axis=0,
        )

    def scores(j, s, queries, low, high):
        keys = kv[0, low:high, lanes(j * DIM, DIM)]
        seen = jnp.concatenate([mask[s, low - s * TOK : high - s * TOK]] * GROUP, axis=1)
        t = jnp.tanh(mm(keys, queries, NT) * (SCALE / CAP))
        return t, jnp.exp(CAP * t) * seen

    def prob_grads(j, grads, low, high):
        return mm(kv[1, low:high, lanes(j * DIM, DIM)], grads, NT)

    def column_sum(a):
        return jnp.sum(a, axis=0, keepdims=True)

    def score_grads(t, probs, dprobs, row_term):
        dscore = probs * (dprobs - row_term) * ((1.0 - t * t) * SCALE)
        return dscore.astype(jnp.bfloat16)

    def far_copy(which, j):
        return remote(
            far_out.at[j, which],
            far_in.at[j, which],
            far_send.at[which, j],
            far_recv.at[which, j],
            device(behind, me),
        )

    def far_out_of(which, j, low, high):
        far_out[j, which, 0:TOK, :] = low[0:TOK].astype(jnp.bfloat16)
        far_out[j, which, TOK:CHIP, :] = (low[TOK:CHIP] + high).astype(jnp.bfloat16)

        @pl.when(has_far)
        def _():
            far_copy(which, j).start()

    def rest_of(which, j, low, high):
        part[j, which] = low[0:CHIP] + high[0:CHIP]
        own_out[j, which, 0:TOK, :] = low[CHIP : CHIP + TOK] + high[CHIP : CHIP + TOK]
        own_out[j, which, TOK:CHIP, :] = high[CHIP + TOK : WINDOW]

    def send_near(which, j):
        for core in range(2):
            remote(
                near_out.at[j, which, core * TOK : (core + 1) * TOK, :],
                near_in.at[which, :, lanes(me * KVW + j * DIM, DIM)],
                near_send.at[which, j],
                near_recv.at[which, me * KVH + j],
                device(behind, core),
            ).start()

    def pass_on(j):
        @pl.when(has_behind)
        def _():
            for which in (1, 0):
                @pl.when(has_ahead)
                def _():
                    wait(far_in.at[j, which], far_recv.at[which, j])

                near_out[j, which] = (
                    part[j, which] + far_in[j, which].astype(jnp.float32)
                ).astype(jnp.bfloat16)
                send_near(which, j)

    def swap(j):
        width = GROUP * DIM
        into = lanes(me * QW + j * width, width)
        cols = lanes(j * width, width)
        remote(
            dq.at[rows(other), cols], dq_out.at[:, into], dq_send.at[j], dq_recv.at[j], partner
        ).start()
        pltpu.make_async_copy(dq.at[rows(me), cols], dq_out.at[:, into], dq_recv.at[j]).start()
        into = lanes(me * KVW + j * DIM, DIM)
        remote(
            own_out.at[j, :, rows(other), :],
            own_in.at[:, :, into],
            part_send.at[j],
            part_recv.at[j],
            partner,
        ).start()
        pltpu.make_async_copy(
            own_out.at[j, :, rows(me), :], own_in.at[:, :, into], part_recv.at[j]
        ).start()

    @pl.loop(0, KVH)
    def _(j):
        queries = [stacked(q, j, s) for s in range(2)]
        grads = [stacked(do, j, s) for s in range(2)]

        near = [scores(j, s, queries[s], CHIP, s * TOK + SPAN) for s in range(2)]
        near_dprobs = [prob_grads(j, grads[s], CHIP, s * TOK + SPAN) for s in range(2)]

        @pl.when(has_far)
        def _():
            wait(head_rows(0, 0, j), relay_recv.at[0, j])

        far = [scores(j, s, queries[s], s * TOK, CHIP) for s in range(2)]
        probs = []
        for s in range(2):
            inverse = 1.0 / (column_sum(far[s][1]) + column_sum(near[s][1]))
            probs.append((far[s][1] * inverse, near[s][1] * inverse))
        low = [[p.astype(jnp.bfloat16) for p in pair] for pair in probs]
        far_out_of(1, j, *(mm(low[s][0], grads[s], NN) for s in range(2)))

        near_terms = [
            column_sum(low[s][1].astype(jnp.float32) * near_dprobs[s]) for s in range(2)
        ]

        @pl.when(has_far)
        def _():
            wait(head_rows(1, 0, j), relay_recv.at[1, j])

        far_low, row_terms = [], []
        for s in range(2):
            dprobs = prob_grads(j, grads[s], s * TOK, CHIP)
            row_terms.append(
                column_sum(low[s][0].astype(jnp.float32) * dprobs) + near_terms[s]
            )
            far_low.append(score_grads(far[s][0], probs[s][0], dprobs, row_terms[s]))
        far_out_of(0, j, *(mm(far_low[s], queries[s], NN) for s in range(2)))

        near_low = [
            score_grads(near[s][0], probs[s][1], near_dprobs[s], row_terms[s]) for s in range(2)
        ]
        rest_of(1, j, *(mm(low[s][1], grads[s], NN) for s in range(2)))
        rest_of(0, j, *(mm(near_low[s], queries[s], NN) for s in range(2)))
        for s in range(2):
            keys = kv[0, s * TOK : s * TOK + SPAN, lanes(j * DIM, DIM)]
            both = jnp.concatenate([far_low[s], near_low[s]], axis=0)
            grad_q = mm(keys, both, TN).T
            for r in range(GROUP):
                dq[s * TOK : (s + 1) * TOK, lanes((j * GROUP + r) * DIM, DIM)] = grad_q[
                    r * TOK : (r + 1) * TOK
                ].astype(jnp.bfloat16)

        swap(j)

        @pl.when(j == 1)
        def _():
            for n in range(2):
                @pl.when(chip > 2)
                def _():
                    relay(n + 2)

                @pl.when(chip != 2)
                def _():
                    pass_on(n)

        @pl.when(j == KVH - 1)
        def _():
            @pl.when(chip == 2)
            def _():
                pass_on(0)
                pass_on(1)

            pass_on(2)
            pass_on(3)

    @pl.when(has_ahead)
    def _():
        wait(seg.at[2:4], seg_send)

    @pl.when(has_behind & has_ahead)
    def _():
        wait(seg.at[2:4], seg_relay_send)

    wait(seg.at[REACH], seg_swap_send)
    for n, (_, dst, _) in enumerate(swaps):
        wait(dst, swap_send.at[n])

    @pl.loop(0, KVH)
    def _(j):
        width = GROUP * DIM
        for which in range(2):
            @pl.when(has_ahead)
            def _():
                wait(head_rows(which, CHIP, j), own_send.at[which, j])

            @pl.when(has_behind & has_ahead)
            def _():
                wait(head_rows(which, 0, j), relay_send.at[which, j])

            @pl.when(has_far)
            def _():
                wait(far_out.at[j, which], far_send.at[which, j])

            @pl.when(has_behind)
            def _():
                wait(near_out.at[j, which], near_send.at[which, j])

        wait(dq.at[0:TOK, lanes(j * width, width)], dq_send.at[j])
        wait(dq.at[:, lanes(j * width, width)], dq_recv.at[j])
        wait(own_out.at[j, :, 0:TOK, :], part_send.at[j])
        wait(own_out.at[j], part_recv.at[j])

        @pl.when(has_ahead)
        def _():
            for which in range(2):
                for core in range(2):
                    wait(
                        near_in.at[which, :, lanes(core * KVW + j * DIM, DIM)],
                        near_recv.at[which, core * KVH + j],
                    )


def finish(dq_in, near_in, own_in, dq_hbm, dk_hbm, dv_hbm, grads, sems):
    dq_copy = pltpu.make_async_copy(dq_in, dq_hbm, sems.at[2])
    dq_copy.start()
    copies = [
        pltpu.make_async_copy(grads.at[n], out, sems.at[n])
        for n, out in enumerate((dk_hbm, dv_hbm))
    ]
    for n in range(2):
        grads[n] = (own_in[n] + near_in[n].astype(jnp.float32)).astype(grads.dtype)
        copies[n].start()
    for copy in (dq_copy, *copies):
        copy.wait()


def local(chips, fsdp, queries, keys, values, grad_out, segment):
    low = jnp.bfloat16
    dma = pltpu.SemaphoreType.DMA
    anywhere = pl.BlockSpec(memory_space=pl.ANY)
    inside = pl.BlockSpec(memory_space=pltpu.VMEM)
    pair = (2, TOK, 2 * KVW)
    parts = pl.pallas_call(
        functools.partial(kernel, chips, fsdp),
        out_shape=(
            pltpu.VMEM((TOK, 2 * QW), low),
            pltpu.VMEM(pair, low),
            pltpu.VMEM(pair, jnp.float32),
        ),
        in_specs=[anywhere] * 5,
        out_specs=(inside,) * 3,
        scratch_shapes=[
            pltpu.VMEM((2, ROWS, KVW), low),
            pltpu.VMEM((CHIP, QW), low),
            pltpu.VMEM((CHIP, QW), low),
            pltpu.VMEM((6, 1, TOK), jnp.int32),
            pltpu.VMEM((2, SPAN, TOK), jnp.float32),
            pltpu.VMEM((KVH, 2, CHIP, DIM), jnp.float32),
            pltpu.VMEM((KVH, 2, CHIP, DIM), jnp.float32),
            pltpu.VMEM((KVH, 2, CHIP, DIM), low),
            pltpu.VMEM((KVH, 2, CHIP, DIM), low),
            pltpu.VMEM((KVH, 2, CHIP, DIM), low),
            pltpu.VMEM((CHIP, QW), low),
            dma((2, KVH)),
            dma((2, KVH)),
            dma((2, KVH)),
            dma((2, KVH)),
            dma((4,)),
            dma((4,)),
            dma(()),
            dma(()),
            dma(()),
            dma(()),
            dma(()),
            dma(()),
            dma((2, KVH)),
            dma((2, KVH)),
            dma((2, KVH)),
            dma((2, 2 * KVH)),
            dma((KVH,)),
            dma((KVH,)),
            dma((KVH,)),
            dma((KVH,)),
            pltpu.SemaphoreType.REGULAR,
        ],
        compiler_params=pltpu.CompilerParams(collective_id=0, has_side_effects=True),
        name="window_grads",
    )(queries, keys, values, grad_out, segment.reshape(1, TOK))
    return pl.pallas_call(
        finish,
        out_shape=tuple(jax.ShapeDtypeStruct(a.shape, low) for a in (queries, keys, values)),
        in_specs=[inside] * 3,
        out_specs=(anywhere,) * 3,
        scratch_shapes=[pltpu.VMEM(pair, low), dma((3,))],
        name="window_grads_out",
    )(*(pltpu.with_memory_space_constraint(part, pltpu.VMEM) for part in parts))


def solution(mesh):
    fsdp = mesh.shape["fsdp"]
    chips = mesh.shape["ctx"] * fsdp // 2
    split = P(("ctx", "fsdp"), None)
    return jax.shard_map(
        functools.partial(local, chips, fsdp),
        mesh=mesh,
        in_specs=(split, split, split, split, P(("ctx", "fsdp"))),
        out_specs=(split, split, split),
        check_vma=False,
    )
```

```python
import functools

import jax
import jax.numpy as jnp
from jax import lax
from jax.experimental import pallas as pl
from jax.experimental.pallas import tpu as pltpu
from jax.sharding import PartitionSpec as P

TOK = 128
DIM = 128
WINDOW = 512
KVH = 4
GROUP = 2
KVW = KVH * DIM
QW = KVW * GROUP
CHIP = 2 * TOK
REACH = WINDOW // TOK
ROWS = WINDOW + CHIP
SPAN = WINDOW + TOK
CAP = 50.0
SCALE = 1.0 / 12.0

NT = (((1,), (1,)), ((), ()))
NN = (((1,), (0,)), ((), ()))
TN = (((0,), (0,)), ((), ()))


def mm(lhs, rhs, dims):
    return lax.dot_general(lhs, rhs, dims, preferred_element_type=jnp.float32)


def kernel(
    chips,
    fsdp,
    q_hbm,
    k_hbm,
    v_hbm,
    do_hbm,
    seg_hbm,
    dq_out,
    near_in,
    own_in,
    kv,
    q,
    do,
    seg,
    mask,
    part,
    own_out,
    far_out,
    far_in,
    near_out,
    dq,
    own_send,
    own_recv,
    relay_send,
    relay_recv,
    swap_send,
    swap_recv,
    seg_send,
    seg_recv,
    seg_swap_send,
    seg_swap_recv,
    seg_relay_send,
    seg_relay_recv,
    far_send,
    far_recv,
    near_send,
    near_recv,
    dq_send,
    dq_recv,
    part_send,
    part_recv,
    ready,
):
    row, column = lax.axis_index("ctx"), lax.axis_index("fsdp")
    me = column % 2
    other = 1 - me
    start = column - me
    row_chips = fsdp // 2
    chip = row * row_chips + start // 2
    partner = (row, start + other)
    rows_all = chips // row_chips
    turns, turned = start == fsdp - 2, start == 0
    ahead = (
        jnp.where(turns, jnp.where(row == rows_all - 1, 0, row + 1), row),
        jnp.where(turns, 0, start + 2),
    )
    behind = (
        jnp.where(turned, jnp.where(row == 0, rows_all - 1, row - 1), row),
        jnp.where(turned, fsdp - 2, start - 2),
    )

    def device(at, core):
        return (at[0], at[1] + core)

    def remote(src, dst, send, recv, to):
        return pltpu.make_async_remote_copy(
            src_ref=src,
            dst_ref=dst,
            send_sem=send,
            recv_sem=recv,
            device_id=to,
            device_id_type=pl.DeviceIdType.MESH,
        )

    def wait(ref, sem):
        pltpu.make_async_copy(ref, ref, sem).wait()

    def lanes(start, size):
        return pl.ds(pl.multiple_of(start, DIM), size)

    def rows(core, base=0):
        return pl.ds(pl.multiple_of(base + core * TOK, TOK), TOK)

    has_ahead = chip < chips - 1
    has_behind = chip > 0
    has_far = chip > 1

    def signal(sem, to):
        pl.semaphore_signal(sem, inc=1, device_id=to, device_id_type=pl.DeviceIdType.MESH)

    barrier = pltpu.get_barrier_semaphore()

    @pl.when(has_behind)
    def _():
        signal(barrier, device(behind, 0))
        signal(barrier, device(behind, 1))

    signal(barrier, partner)
    pl.semaphore_wait(barrier, 1 + 2 * jnp.where(has_ahead, 1, 0))

    @pl.when(has_ahead)
    def _():
        signal(ready, device(ahead, 0))
        signal(ready, device(ahead, 1))

    def send_own(j):
        @pl.when(has_ahead)
        def _():
            for which, src in ((0, k_hbm), (1, v_hbm)):
                for core in range(2):
                    remote(
                        src.at[:, lanes(core * KVW + j * DIM, DIM)],
                        kv.at[which, rows(me, CHIP), lanes(j * DIM, DIM)],
                        own_send.at[which, j],
                        own_recv.at[which, j],
                        device(ahead, core),
                    ).start()

    def head_rows(which, start, j):
        return kv.at[which, start : start + CHIP, lanes(j * DIM, DIM)]

    def relay_one(which, j):
        @pl.when(has_behind)
        def _():
            wait(head_rows(which, CHIP, j), own_recv.at[which, j])

        @pl.when(has_behind & has_ahead)
        def _():
            remote(
                head_rows(which, CHIP, j),
                head_rows(which, 0, j),
                relay_send.at[which, j],
                relay_recv.at[which, j],
                device(ahead, me),
            ).start()

    def relay(j):
        for which in range(2):
            relay_one(which, j)

    @pl.when(has_ahead)
    def _():
        for core in range(2):
            remote(seg_hbm, seg.at[2 + me], seg_send, seg_recv, device(ahead, core)).start()

    send_own(0)
    send_own(1)

    @pl.when(chip <= 1)
    def _():
        send_own(2)
        send_own(3)

    remote(seg_hbm, seg.at[REACH + me], seg_swap_send, seg_swap_recv, partner).start()
    pltpu.make_async_copy(seg_hbm, seg.at[REACH + me], seg_swap_recv).start()
    swaps = (
        (k_hbm, kv.at[0, rows(me, WINDOW), :], KVW),
        (v_hbm, kv.at[1, rows(me, WINDOW), :], KVW),
        (q_hbm, q.at[rows(me), :], QW),
        (do_hbm, do.at[rows(me), :], QW),
    )
    for n, (src, dst, width) in enumerate(swaps):
        remote(
            src.at[:, lanes(other * width, width)],
            dst,
            swap_send.at[n],
            swap_recv.at[n],
            partner,
        ).start()
        pltpu.make_async_copy(
            src.at[:, lanes(me * width, width)], dst, swap_recv.at[n]
        ).start()

    @pl.when(chip <= 1)
    def _():
        kv[:, 0:CHIP, :] = jnp.zeros((2, CHIP, KVW), kv.dtype)
        seg[0:2] = jnp.zeros((2, 1, TOK), seg.dtype)

    @pl.when(chip == 0)
    def _():
        kv[:, CHIP:WINDOW, :] = jnp.zeros((2, CHIP, KVW), kv.dtype)
        seg[2:4] = jnp.zeros((2, 1, TOK), seg.dtype)

    @pl.when(chip == chips - 1)
    def _():
        far_in[...] = jnp.zeros(far_in.shape, far_in.dtype)
        near_in[...] = jnp.zeros(near_in.shape, near_in.dtype)

    @pl.when(has_behind)
    def _():
        wait(seg.at[2:4], seg_recv)

    @pl.when(has_behind & has_ahead)
    def _():
        remote(
            seg.at[2:4], seg.at[0:2], seg_relay_send, seg_relay_recv, device(ahead, me)
        ).start()

    relay(0)
    relay(1)

    @pl.when(chip > 1)
    def _():
        send_own(2)
        send_own(3)

    @pl.when(chip <= 2)
    def _():
        relay(2)
        relay(3)

    wait(seg.at[4:6], seg_swap_recv)

    @pl.when(has_far)
    def _():
        wait(seg.at[0:2], seg_relay_recv)

    @pl.when(has_behind)
    def _():
        pl.semaphore_wait(ready, 2)

    key_at = lax.broadcasted_iota(jnp.int32, (TOK, TOK), 0)
    query_at = lax.broadcasted_iota(jnp.int32, (TOK, TOK), 1)
    for b in range(6):
        wide = jnp.broadcast_to(seg[b].astype(jnp.float32), (TOK, TOK))
        key_seg = wide.T
        real = jnp.where(2 * chip - REACH + b >= 0, 1.0, 0.0)
        for s in range(2):
            distance = REACH + s - b
            if distance < 0 or distance > REACH:
                continue
            query_seg = jnp.broadcast_to(seg[REACH + s].astype(jnp.float32), (TOK, TOK))
            seen = jnp.where(key_seg == query_seg, real, 0.0)
            if distance == 0:
                seen = jnp.where(query_at >= key_at, seen, 0.0)
            if distance == REACH:
                seen = jnp.where(query_at < key_at, seen, 0.0)
            at = (b - s) * TOK
            mask[s, at : at + TOK, :] = seen

    wait(kv.at[0, WINDOW:ROWS, :], swap_recv.at[0])
    wait(kv.at[1, WINDOW:ROWS, :], swap_recv.at[1])
    wait(q, swap_recv.at[2])
    wait(do, swap_recv.at[3])

    def stacked(ref, j, s):
        return jnp.concatenate(
            [
                ref[s * TOK : (s + 1) * TOK, lanes((j * GROUP + r) * DIM, DIM)]
                for r in range(GROUP)
            ],
            axis=0,
        )

    def scores(j, s, queries, low, high):
        keys = kv[0, low:high, lanes(j * DIM, DIM)]
        seen = jnp.concatenate([mask[s, low - s * TOK : high - s * TOK]] * GROUP, axis=1)
        t = jnp.tanh(mm(keys, queries, NT) * (SCALE / CAP))
        return t, jnp.exp(CAP * t) * seen

    def prob_grads(j, grads, low, high):
        return mm(kv[1, low:high, lanes(j * DIM, DIM)], grads, NT)

    def column_sum(a):
        return jnp.sum(a, axis=0, keepdims=True)

    def score_grads(t, probs, dprobs, row_term):
        dscore = probs * (dprobs - row_term) * ((1.0 - t * t) * SCALE)
        return dscore.astype(jnp.bfloat16)

    def far_copy(which, j):
        return remote(
            far_out.at[j, which],
            far_in.at[j, which],
            far_send.at[which, j],
            far_recv.at[which, j],
            device(behind, me),
        )

    def far_out_of(which, j, low, high):
        far_out[j, which, 0:TOK, :] = low[0:TOK].astype(jnp.bfloat16)
        far_out[j, which, TOK:CHIP, :] = (low[TOK:CHIP] + high).astype(jnp.bfloat16)

        @pl.when(has_far)
        def _():
            far_copy(which, j).start()

    def rest_of(which, j, low, high):
        part[j, which] = low[0:CHIP] + high[0:CHIP]
        own_out[j, which, 0:TOK, :] = low[CHIP : CHIP + TOK] + high[CHIP : CHIP + TOK]
        own_out[j, which, TOK:CHIP, :] = high[CHIP + TOK : WINDOW]

    def send_near(which, j):
        for core in range(2):
            remote(
                near_out.at[j, which, core * TOK : (core + 1) * TOK, :],
                near_in.at[which, :, lanes(me * KVW + j * DIM, DIM)],
                near_send.at[which, j],
                near_recv.at[which, me * KVH + j],
                device(behind, core),
            ).start()

    def pass_one(which, j):
        @pl.when(has_behind)
        def _():
            @pl.when(has_ahead)
            def _():
                wait(far_in.at[j, which], far_recv.at[which, j])

            near_out[j, which] = (
                part[j, which] + far_in[j, which].astype(jnp.float32)
            ).astype(jnp.bfloat16)
            send_near(which, j)

    def pass_on(j):
        for which in (1, 0):
            pass_one(which, j)

    def swap(j):
        width = GROUP * DIM
        into = lanes(me * QW + j * width, width)
        cols = lanes(j * width, width)
        remote(
            dq.at[rows(other), cols], dq_out.at[:, into], dq_send.at[j], dq_recv.at[j], partner
        ).start()
        pltpu.make_async_copy(dq.at[rows(me), cols], dq_out.at[:, into], dq_recv.at[j]).start()
        into = lanes(me * KVW + j * DIM, DIM)
        remote(
            own_out.at[j, :, rows(other), :],
            own_in.at[:, :, into],
            part_send.at[j],
            part_recv.at[j],
            partner,
        ).start()
        pltpu.make_async_copy(
            own_out.at[j, :, rows(me), :], own_in.at[:, :, into], part_recv.at[j]
        ).start()

    @pl.loop(0, KVH)
    def _(j):
        queries = [stacked(q, j, s) for s in range(2)]
        grads = [stacked(do, j, s) for s in range(2)]

        near = [scores(j, s, queries[s], CHIP, s * TOK + SPAN) for s in range(2)]
        near_dprobs = [prob_grads(j, grads[s], CHIP, s * TOK + SPAN) for s in range(2)]

        @pl.when(has_far)
        def _():
            wait(head_rows(0, 0, j), relay_recv.at[0, j])

        far = [scores(j, s, queries[s], s * TOK, CHIP) for s in range(2)]
        probs = []
        for s in range(2):
            inverse = 1.0 / (column_sum(far[s][1]) + column_sum(near[s][1]))
            probs.append((far[s][1] * inverse, near[s][1] * inverse))
        low = [[p.astype(jnp.bfloat16) for p in pair] for pair in probs]
        far_out_of(1, j, *(mm(low[s][0], grads[s], NN) for s in range(2)))

        near_terms = [
            column_sum(low[s][1].astype(jnp.float32) * near_dprobs[s]) for s in range(2)
        ]

        @pl.when(has_far)
        def _():
            wait(head_rows(1, 0, j), relay_recv.at[1, j])

        far_low, row_terms = [], []
        for s in range(2):
            dprobs = prob_grads(j, grads[s], s * TOK, CHIP)
            row_terms.append(
                column_sum(low[s][0].astype(jnp.float32) * dprobs) + near_terms[s]
            )
            far_low.append(score_grads(far[s][0], probs[s][0], dprobs, row_terms[s]))
        far_out_of(0, j, *(mm(far_low[s], queries[s], NN) for s in range(2)))

        near_low = [
            score_grads(near[s][0], probs[s][1], near_dprobs[s], row_terms[s]) for s in range(2)
        ]
        rest_of(1, j, *(mm(low[s][1], grads[s], NN) for s in range(2)))
        rest_of(0, j, *(mm(near_low[s], queries[s], NN) for s in range(2)))
        for s in range(2):
            keys = kv[0, s * TOK : s * TOK + SPAN, lanes(j * DIM, DIM)]
            both = jnp.concatenate([far_low[s], near_low[s]], axis=0)
            grad_q = mm(keys, both, TN).T
            for r in range(GROUP):
                dq[s * TOK : (s + 1) * TOK, lanes((j * GROUP + r) * DIM, DIM)] = grad_q[
                    r * TOK : (r + 1) * TOK
                ].astype(jnp.bfloat16)

        swap(j)

        @pl.when(chip <= 1)
        def _():
            pass_on(j)

        @pl.when((j == 1) & (chip > 2))
        def _():
            for n in range(2):
                for which in range(2):
                    relay_one(which, n + 2)
                    pass_one(1 - which, n)

        @pl.when((j == KVH - 1) & (chip > 1))
        def _():
            @pl.when(chip == 2)
            def _():
                pass_on(0)
                pass_on(1)

            pass_on(2)
            pass_on(3)

    @pl.when(has_ahead)
    def _():
        wait(seg.at[2:4], seg_send)

    @pl.when(has_behind & has_ahead)
    def _():
        wait(seg.at[2:4], seg_relay_send)

    wait(seg.at[REACH], seg_swap_send)
    for n, (_, dst, _) in enumerate(swaps):
        wait(dst, swap_send.at[n])

    @pl.loop(0, KVH)
    def _(j):
        width = GROUP * DIM
        for which in range(2):
            @pl.when(has_ahead)
            def _():
                wait(head_rows(which, CHIP, j), own_send.at[which, j])

            @pl.when(has_behind & has_ahead)
            def _():
                wait(head_rows(which, 0, j), relay_send.at[which, j])

            @pl.when(has_far)
            def _():
                wait(far_out.at[j, which], far_send.at[which, j])

            @pl.when(has_behind)
            def _():
                wait(near_out.at[j, which], near_send.at[which, j])

        wait(dq.at[0:TOK, lanes(j * width, width)], dq_send.at[j])
        wait(dq.at[:, lanes(j * width, width)], dq_recv.at[j])
        wait(own_out.at[j, :, 0:TOK, :], part_send.at[j])
        wait(own_out.at[j], part_recv.at[j])

        @pl.when(has_ahead)
        def _():
            for which in range(2):
                for core in range(2):
                    wait(
                        near_in.at[which, :, lanes(core * KVW + j * DIM, DIM)],
                        near_recv.at[which, core * KVH + j],
                    )


def finish(dq_in, near_in, own_in, dq_hbm, dk_hbm, dv_hbm, grads, sems):
    dq_copy = pltpu.make_async_copy(dq_in, dq_hbm, sems.at[2])
    dq_copy.start()
    copies = [
        pltpu.make_async_copy(grads.at[n], out, sems.at[n])
        for n, out in enumerate((dk_hbm, dv_hbm))
    ]
    for n in range(2):
        grads[n] = (own_in[n] + near_in[n].astype(jnp.float32)).astype(grads.dtype)
        copies[n].start()
    for copy in (dq_copy, *copies):
        copy.wait()


def local(chips, fsdp, queries, keys, values, grad_out, segment):
    low = jnp.bfloat16
    dma = pltpu.SemaphoreType.DMA
    anywhere = pl.BlockSpec(memory_space=pl.ANY)
    inside = pl.BlockSpec(memory_space=pltpu.VMEM)
    pair = (2, TOK, 2 * KVW)
    parts = pl.pallas_call(
        functools.partial(kernel, chips, fsdp),
        out_shape=(
            pltpu.VMEM((TOK, 2 * QW), low),
            pltpu.VMEM(pair, low),
            pltpu.VMEM(pair, jnp.float32),
        ),
        in_specs=[anywhere] * 5,
        out_specs=(inside,) * 3,
        scratch_shapes=[
            pltpu.VMEM((2, ROWS, KVW), low),
            pltpu.VMEM((CHIP, QW), low),
            pltpu.VMEM((CHIP, QW), low),
            pltpu.VMEM((6, 1, TOK), jnp.int32),
            pltpu.VMEM((2, SPAN, TOK), jnp.float32),
            pltpu.VMEM((KVH, 2, CHIP, DIM), jnp.float32),
            pltpu.VMEM((KVH, 2, CHIP, DIM), jnp.float32),
            pltpu.VMEM((KVH, 2, CHIP, DIM), low),
            pltpu.VMEM((KVH, 2, CHIP, DIM), low),
            pltpu.VMEM((KVH, 2, CHIP, DIM), low),
            pltpu.VMEM((CHIP, QW), low),
            dma((2, KVH)),
            dma((2, KVH)),
            dma((2, KVH)),
            dma((2, KVH)),
            dma((4,)),
            dma((4,)),
            dma(()),
            dma(()),
            dma(()),
            dma(()),
            dma(()),
            dma(()),
            dma((2, KVH)),
            dma((2, KVH)),
            dma((2, KVH)),
            dma((2, 2 * KVH)),
            dma((KVH,)),
            dma((KVH,)),
            dma((KVH,)),
            dma((KVH,)),
            pltpu.SemaphoreType.REGULAR,
        ],
        compiler_params=pltpu.CompilerParams(collective_id=0, has_side_effects=True),
        name="window_grads",
    )(queries, keys, values, grad_out, segment.reshape(1, TOK))
    return pl.pallas_call(
        finish,
        out_shape=tuple(jax.ShapeDtypeStruct(a.shape, low) for a in (queries, keys, values)),
        in_specs=[inside] * 3,
        out_specs=(anywhere,) * 3,
        scratch_shapes=[pltpu.VMEM(pair, low), dma((3,))],
        name="window_grads_out",
    )(*(pltpu.with_memory_space_constraint(part, pltpu.VMEM) for part in parts))


def solution(mesh):
    fsdp = mesh.shape["fsdp"]
    chips = mesh.shape["ctx"] * fsdp // 2
    split = P(("ctx", "fsdp"), None)
    return jax.shard_map(
        functools.partial(local, chips, fsdp),
        mesh=mesh,
        in_specs=(split, split, split, split, P(("ctx", "fsdp"))),
        out_specs=(split, split, split),
        check_vma=False,
    )
```

```python
import functools

import jax
import jax.numpy as jnp
from jax import lax
from jax.experimental import pallas as pl
from jax.experimental.pallas import tpu as pltpu
from jax.sharding import PartitionSpec as P

TOK = 128
DIM = 128
WINDOW = 512
KVH = 4
GROUP = 2
KVW = KVH * DIM
QW = KVW * GROUP
CHIP = 2 * TOK
REACH = WINDOW // TOK
ROWS = WINDOW + CHIP
SPAN = WINDOW + TOK
CAP = 50.0
SCALE = 1.0 / 12.0

NT = (((1,), (1,)), ((), ()))
NN = (((1,), (0,)), ((), ()))
TN = (((0,), (0,)), ((), ()))


def mm(lhs, rhs, dims):
    return lax.dot_general(lhs, rhs, dims, preferred_element_type=jnp.float32)


def kernel(
    chips,
    fsdp,
    q_hbm,
    k_hbm,
    v_hbm,
    do_hbm,
    seg_hbm,
    dq_out,
    near_in,
    own_in,
    kv,
    q,
    do,
    seg,
    mask,
    part,
    own_out,
    far_out,
    far_in,
    near_out,
    dq,
    own_send,
    own_recv,
    relay_send,
    relay_recv,
    swap_send,
    swap_recv,
    seg_send,
    seg_recv,
    seg_swap_send,
    seg_swap_recv,
    seg_relay_send,
    seg_relay_recv,
    far_send,
    far_recv,
    near_send,
    near_recv,
    dq_send,
    dq_recv,
    part_send,
    part_recv,
    ready,
):
    row, column = lax.axis_index("ctx"), lax.axis_index("fsdp")
    me = column % 2
    other = 1 - me
    start = column - me
    row_chips = fsdp // 2
    chip = row * row_chips + start // 2
    partner = (row, start + other)
    rows_all = chips // row_chips
    turns, turned = start == fsdp - 2, start == 0
    ahead = (
        jnp.where(turns, jnp.where(row == rows_all - 1, 0, row + 1), row),
        jnp.where(turns, 0, start + 2),
    )
    behind = (
        jnp.where(turned, jnp.where(row == 0, rows_all - 1, row - 1), row),
        jnp.where(turned, fsdp - 2, start - 2),
    )

    def device(at, core):
        return (at[0], at[1] + core)

    def remote(src, dst, send, recv, to):
        return pltpu.make_async_remote_copy(
            src_ref=src,
            dst_ref=dst,
            send_sem=send,
            recv_sem=recv,
            device_id=to,
            device_id_type=pl.DeviceIdType.MESH,
        )

    def wait(ref, sem):
        pltpu.make_async_copy(ref, ref, sem).wait()

    def lanes(start, size):
        return pl.ds(pl.multiple_of(start, DIM), size)

    def rows(core, base=0):
        return pl.ds(pl.multiple_of(base + core * TOK, TOK), TOK)

    has_ahead = chip < chips - 1
    has_behind = chip > 0
    has_far = chip > 1

    def signal(sem, to):
        pl.semaphore_signal(sem, inc=1, device_id=to, device_id_type=pl.DeviceIdType.MESH)

    barrier = pltpu.get_barrier_semaphore()

    @pl.when(has_behind)
    def _():
        signal(barrier, device(behind, 0))
        signal(barrier, device(behind, 1))

    signal(barrier, partner)
    pl.semaphore_wait(barrier, 1 + 2 * jnp.where(has_ahead, 1, 0))

    @pl.when(has_ahead)
    def _():
        signal(ready, device(ahead, 0))
        signal(ready, device(ahead, 1))

    def send_own(j):
        @pl.when(has_ahead)
        def _():
            for which, src in ((0, k_hbm), (1, v_hbm)):
                for core in range(2):
                    remote(
                        src.at[:, lanes(core * KVW + j * DIM, DIM)],
                        kv.at[which, rows(me, CHIP), lanes(j * DIM, DIM)],
                        own_send.at[which, j],
                        own_recv.at[which, j],
                        device(ahead, core),
                    ).start()

    def head_rows(which, start, j):
        return kv.at[which, start : start + CHIP, lanes(j * DIM, DIM)]

    def relay_one(which, j):
        @pl.when(has_behind)
        def _():
            wait(head_rows(which, CHIP, j), own_recv.at[which, j])

        @pl.when(has_behind & has_ahead)
        def _():
            remote(
                head_rows(which, CHIP, j),
                head_rows(which, 0, j),
                relay_send.at[which, j],
                relay_recv.at[which, j],
                device(ahead, me),
            ).start()

    def relay(j):
        for which in range(2):
            relay_one(which, j)

    @pl.when(has_ahead)
    def _():
        for core in range(2):
            remote(seg_hbm, seg.at[2 + me], seg_send, seg_recv, device(ahead, core)).start()

    send_own(0)
    send_own(1)

    @pl.when(chip <= 1)
    def _():
        send_own(2)
        send_own(3)

    remote(seg_hbm, seg.at[REACH + me], seg_swap_send, seg_swap_recv, partner).start()
    pltpu.make_async_copy(seg_hbm, seg.at[REACH + me], seg_swap_recv).start()
    swaps = (
        (k_hbm, kv.at[0, rows(me, WINDOW), :], KVW),
        (v_hbm, kv.at[1, rows(me, WINDOW), :], KVW),
        (q_hbm, q.at[rows(me), :], QW),
        (do_hbm, do.at[rows(me), :], QW),
    )
    for n, (src, dst, width) in enumerate(swaps):
        remote(
            src.at[:, lanes(other * width, width)],
            dst,
            swap_send.at[n],
            swap_recv.at[n],
            partner,
        ).start()
        pltpu.make_async_copy(
            src.at[:, lanes(me * width, width)], dst, swap_recv.at[n]
        ).start()

    @pl.when(chip <= 1)
    def _():
        kv[:, 0:CHIP, :] = jnp.zeros((2, CHIP, KVW), kv.dtype)
        seg[0:2] = jnp.zeros((2, 1, TOK), seg.dtype)

    @pl.when(chip == 0)
    def _():
        kv[:, CHIP:WINDOW, :] = jnp.zeros((2, CHIP, KVW), kv.dtype)
        seg[2:4] = jnp.zeros((2, 1, TOK), seg.dtype)

    @pl.when(chip == chips - 1)
    def _():
        far_in[...] = jnp.zeros(far_in.shape, far_in.dtype)
        near_in[...] = jnp.zeros(near_in.shape, near_in.dtype)

    @pl.when(has_behind)
    def _():
        wait(seg.at[2:4], seg_recv)

    @pl.when(has_behind & has_ahead)
    def _():
        remote(
            seg.at[2:4], seg.at[0:2], seg_relay_send, seg_relay_recv, device(ahead, me)
        ).start()

    relay(0)
    relay(1)

    @pl.when(chip > 1)
    def _():
        send_own(2)
        send_own(3)

    @pl.when(chip <= 2)
    def _():
        relay(2)
        relay(3)

    wait(seg.at[4:6], seg_swap_recv)

    @pl.when(has_far)
    def _():
        wait(seg.at[0:2], seg_relay_recv)

    @pl.when(has_behind)
    def _():
        pl.semaphore_wait(ready, 2)

    key_at = lax.broadcasted_iota(jnp.int32, (TOK, TOK), 0)
    query_at = lax.broadcasted_iota(jnp.int32, (TOK, TOK), 1)
    for b in range(6):
        wide = jnp.broadcast_to(seg[b].astype(jnp.float32), (TOK, TOK))
        key_seg = wide.T
        real = jnp.where(2 * chip - REACH + b >= 0, 1.0, 0.0)
        for s in range(2):
            distance = REACH + s - b
            if distance < 0 or distance > REACH:
                continue
            query_seg = jnp.broadcast_to(seg[REACH + s].astype(jnp.float32), (TOK, TOK))
            seen = jnp.where(key_seg == query_seg, real, 0.0)
            if distance == 0:
                seen = jnp.where(query_at >= key_at, seen, 0.0)
            if distance == REACH:
                seen = jnp.where(query_at < key_at, seen, 0.0)
            at = (b - s) * TOK
            mask[s, at : at + TOK, :] = seen

    wait(kv.at[0, WINDOW:ROWS, :], swap_recv.at[0])
    wait(kv.at[1, WINDOW:ROWS, :], swap_recv.at[1])
    wait(q, swap_recv.at[2])
    wait(do, swap_recv.at[3])

    def stacked(ref, j, s):
        return jnp.concatenate(
            [
                ref[s * TOK : (s + 1) * TOK, lanes((j * GROUP + r) * DIM, DIM)]
                for r in range(GROUP)
            ],
            axis=0,
        )

    def scores(j, s, queries, low, high):
        keys = kv[0, low:high, lanes(j * DIM, DIM)]
        seen = jnp.concatenate([mask[s, low - s * TOK : high - s * TOK]] * GROUP, axis=1)
        t = jnp.tanh(mm(keys, queries, NT) * (SCALE / CAP))
        return t, jnp.exp(CAP * t) * seen

    def prob_grads(j, grads, low, high):
        return mm(kv[1, low:high, lanes(j * DIM, DIM)], grads, NT)

    def column_sum(a):
        return jnp.sum(a, axis=0, keepdims=True)

    def score_grads(t, probs, dprobs, row_term):
        dscore = probs * (dprobs - row_term) * ((1.0 - t * t) * SCALE)
        return dscore.astype(jnp.bfloat16)

    def far_copy(which, j):
        return remote(
            far_out.at[j, which],
            far_in.at[j, which],
            far_send.at[which, j],
            far_recv.at[which, j],
            device(behind, me),
        )

    def far_out_of(which, j, low, high):
        far_out[j, which, 0:TOK, :] = low[0:TOK].astype(jnp.bfloat16)
        far_out[j, which, TOK:CHIP, :] = (low[TOK:CHIP] + high).astype(jnp.bfloat16)

        @pl.when(has_far)
        def _():
            far_copy(which, j).start()

    def rest_of(which, j, low, high):
        part[j, which] = low[0:CHIP] + high[0:CHIP]
        own_out[j, which, 0:TOK, :] = low[CHIP : CHIP + TOK] + high[CHIP : CHIP + TOK]
        own_out[j, which, TOK:CHIP, :] = high[CHIP + TOK : WINDOW]

    def send_near(which, j):
        for core in range(2):
            remote(
                near_out.at[j, which, core * TOK : (core + 1) * TOK, :],
                near_in.at[which, :, lanes(me * KVW + j * DIM, DIM)],
                near_send.at[which, j],
                near_recv.at[which, me * KVH + j],
                device(behind, core),
            ).start()

    def pass_one(which, j):
        @pl.when(has_behind)
        def _():
            @pl.when(has_ahead)
            def _():
                wait(far_in.at[j, which], far_recv.at[which, j])

            near_out[j, which] = (
                part[j, which] + far_in[j, which].astype(jnp.float32)
            ).astype(jnp.bfloat16)
            send_near(which, j)

    def pass_on(j):
        for which in (1, 0):
            pass_one(which, j)

    def swap(j):
        width = GROUP * DIM
        into = lanes(me * QW + j * width, width)
        cols = lanes(j * width, width)
        remote(
            dq.at[rows(other), cols], dq_out.at[:, into], dq_send.at[j], dq_recv.at[j], partner
        ).start()
        pltpu.make_async_copy(dq.at[rows(me), cols], dq_out.at[:, into], dq_recv.at[j]).start()
        into = lanes(me * KVW + j * DIM, DIM)
        remote(
            own_out.at[j, :, rows(other), :],
            own_in.at[:, :, into],
            part_send.at[j],
            part_recv.at[j],
            partner,
        ).start()
        pltpu.make_async_copy(
            own_out.at[j, :, rows(me), :], own_in.at[:, :, into], part_recv.at[j]
        ).start()

    @pl.loop(0, KVH)
    def _(j):
        queries = [stacked(q, j, s) for s in range(2)]
        grads = [stacked(do, j, s) for s in range(2)]

        near = [scores(j, s, queries[s], CHIP, s * TOK + SPAN) for s in range(2)]
        near_dprobs = [prob_grads(j, grads[s], CHIP, s * TOK + SPAN) for s in range(2)]

        @pl.when(has_far)
        def _():
            wait(head_rows(0, 0, j), relay_recv.at[0, j])

        far = [scores(j, s, queries[s], s * TOK, CHIP) for s in range(2)]
        probs = []
        for s in range(2):
            inverse = 1.0 / (column_sum(far[s][1]) + column_sum(near[s][1]))
            probs.append((far[s][1] * inverse, near[s][1] * inverse))
        low = [[p.astype(jnp.bfloat16) for p in pair] for pair in probs]
        far_out_of(1, j, *(mm(low[s][0], grads[s], NN) for s in range(2)))

        near_terms = [
            column_sum(low[s][1].astype(jnp.float32) * near_dprobs[s]) for s in range(2)
        ]

        @pl.when(has_far)
        def _():
            wait(head_rows(1, 0, j), relay_recv.at[1, j])

        far_low, row_terms = [], []
        for s in range(2):
            dprobs = prob_grads(j, grads[s], s * TOK, CHIP)
            row_terms.append(
                column_sum(low[s][0].astype(jnp.float32) * dprobs) + near_terms[s]
            )
            far_low.append(score_grads(far[s][0], probs[s][0], dprobs, row_terms[s]))
        far_out_of(0, j, *(mm(far_low[s], queries[s], NN) for s in range(2)))

        near_low = [
            score_grads(near[s][0], probs[s][1], near_dprobs[s], row_terms[s]) for s in range(2)
        ]
        rest_of(1, j, *(mm(low[s][1], grads[s], NN) for s in range(2)))
        rest_of(0, j, *(mm(near_low[s], queries[s], NN) for s in range(2)))
        for s in range(2):
            keys = kv[0, s * TOK : s * TOK + SPAN, lanes(j * DIM, DIM)]
            both = jnp.concatenate([far_low[s], near_low[s]], axis=0)
            grad_q = mm(keys, both, TN).T
            for r in range(GROUP):
                dq[s * TOK : (s + 1) * TOK, lanes((j * GROUP + r) * DIM, DIM)] = grad_q[
                    r * TOK : (r + 1) * TOK
                ].astype(jnp.bfloat16)

        swap(j)

        @pl.when(chip <= 1)
        def _():
            pass_on(j)

        @pl.when((j == 1) & (chip > 2))
        def _():
            for n in range(2):
                for which in range(2):
                    relay_one(which, n + 2)
                    pass_one(1 - which, n)

        @pl.when((j == KVH - 1) & (chip > 1))
        def _():
            @pl.when(chip == 2)
            def _():
                pass_on(0)
                pass_on(1)

            pass_on(2)
            pass_on(3)

    @pl.when(has_ahead)
    def _():
        wait(seg.at[2:4], seg_send)

    @pl.when(has_behind & has_ahead)
    def _():
        wait(seg.at[2:4], seg_relay_send)

    wait(seg.at[REACH], seg_swap_send)
    for n, (_, dst, _) in enumerate(swaps):
        wait(dst, swap_send.at[n])

    @pl.loop(0, KVH)
    def _(j):
        width = GROUP * DIM
        for which in range(2):
            @pl.when(has_ahead)
            def _():
                wait(head_rows(which, CHIP, j), own_send.at[which, j])

            @pl.when(has_behind & has_ahead)
            def _():
                wait(head_rows(which, 0, j), relay_send.at[which, j])

            @pl.when(has_far)
            def _():
                wait(far_out.at[j, which], far_send.at[which, j])

            @pl.when(has_behind)
            def _():
                wait(near_out.at[j, which], near_send.at[which, j])

        wait(dq.at[0:TOK, lanes(j * width, width)], dq_send.at[j])
        wait(dq.at[:, lanes(j * width, width)], dq_recv.at[j])
        wait(own_out.at[j, :, 0:TOK, :], part_send.at[j])
        wait(own_out.at[j], part_recv.at[j])

        @pl.when(has_ahead)
        def _():
            for which in range(2):
                for core in range(2):
                    wait(
                        near_in.at[which, :, lanes(core * KVW + j * DIM, DIM)],
                        near_recv.at[which, core * KVH + j],
                    )


def finish(dq_in, near_in, own_in, dq_hbm, dk_hbm, dv_hbm, grads, sems):
    dq_copy = pltpu.make_async_copy(dq_in, dq_hbm, sems.at[4])
    dq_copy.start()
    copies = []
    for n, out in enumerate((dk_hbm, dv_hbm)):
        for half in range(2):
            at = pl.ds(half * TOK // 2, TOK // 2)
            grads[n, at, :] = (
                own_in[n, at, :] + near_in[n, at, :].astype(jnp.float32)
            ).astype(grads.dtype)
            copy = pltpu.make_async_copy(
                grads.at[n, at, :], out.at[at, :], sems.at[2 * n + half]
            )
            copy.start()
            copies.append(copy)
    for copy in (dq_copy, *copies):
        copy.wait()


def local(chips, fsdp, queries, keys, values, grad_out, segment):
    low = jnp.bfloat16
    dma = pltpu.SemaphoreType.DMA
    anywhere = pl.BlockSpec(memory_space=pl.ANY)
    inside = pl.BlockSpec(memory_space=pltpu.VMEM)
    pair = (2, TOK, 2 * KVW)
    parts = pl.pallas_call(
        functools.partial(kernel, chips, fsdp),
        out_shape=(
            pltpu.VMEM((TOK, 2 * QW), low),
            pltpu.VMEM(pair, low),
            pltpu.VMEM(pair, jnp.float32),
        ),
        in_specs=[anywhere] * 5,
        out_specs=(inside,) * 3,
        scratch_shapes=[
            pltpu.VMEM((2, ROWS, KVW), low),
            pltpu.VMEM((CHIP, QW), low),
            pltpu.VMEM((CHIP, QW), low),
            pltpu.VMEM((6, 1, TOK), jnp.int32),
            pltpu.VMEM((2, SPAN, TOK), jnp.float32),
            pltpu.VMEM((KVH, 2, CHIP, DIM), jnp.float32),
            pltpu.VMEM((KVH, 2, CHIP, DIM), jnp.float32),
            pltpu.VMEM((KVH, 2, CHIP, DIM), low),
            pltpu.VMEM((KVH, 2, CHIP, DIM), low),
            pltpu.VMEM((KVH, 2, CHIP, DIM), low),
            pltpu.VMEM((CHIP, QW), low),
            dma((2, KVH)),
            dma((2, KVH)),
            dma((2, KVH)),
            dma((2, KVH)),
            dma((4,)),
            dma((4,)),
            dma(()),
            dma(()),
            dma(()),
            dma(()),
            dma(()),
            dma(()),
            dma((2, KVH)),
            dma((2, KVH)),
            dma((2, KVH)),
            dma((2, 2 * KVH)),
            dma((KVH,)),
            dma((KVH,)),
            dma((KVH,)),
            dma((KVH,)),
            pltpu.SemaphoreType.REGULAR,
        ],
        compiler_params=pltpu.CompilerParams(collective_id=0, has_side_effects=True),
        name="window_grads",
    )(queries, keys, values, grad_out, segment.reshape(1, TOK))
    return pl.pallas_call(
        finish,
        out_shape=tuple(jax.ShapeDtypeStruct(a.shape, low) for a in (queries, keys, values)),
        in_specs=[inside] * 3,
        out_specs=(anywhere,) * 3,
        scratch_shapes=[pltpu.VMEM(pair, low), dma((5,))],
        name="window_grads_out",
    )(*(pltpu.with_memory_space_constraint(part, pltpu.VMEM) for part in parts))


def solution(mesh):
    fsdp = mesh.shape["fsdp"]
    chips = mesh.shape["ctx"] * fsdp // 2
    split = P(("ctx", "fsdp"), None)
    return jax.shard_map(
        functools.partial(local, chips, fsdp),
        mesh=mesh,
        in_specs=(split, split, split, split, P(("ctx", "fsdp"))),
        out_specs=(split, split, split),
        check_vma=False,
    )
```
